256 devices in a mesh: env: 4 (over x), wave: 64 (over y, z, core).
Axes of the slice: x: 4, y: 4, z: 8, core: 2. Of those that a mesh axis runs over, the one named last changes fastest.
Arguments:
- psi: bfloat16 [4096, 128, 128], P('wave'), may hold values from -6 to 6
- left_env: bfloat16 [40, 64, 128, 128], P('env', 'wave'), may hold values from -0.5 to 0.5
- right_env: bfloat16 [40, 64, 128, 128], P('env', 'wave'), may hold values from -0.078125 to 0.078125
- left_sector: int32 [4096, 1], P('wave'), may hold values from 0 to 63; in each aligned block of 64 rows (0 to 63, 64 to 127, ...) at most 2 rows name the same one
- right_sector: int32 [4096, 1], P('wave'), may hold values from 0 to 63
- sector_owner: int32 [64], replicated, may hold values from 0 to 63, each once
- sector_rows: int32 [64], replicated, may hold values from 64 to 128
Outputs:
- h_psi: bfloat16 [4096, 128, 128], P('wave', 'env')
The draws below stay inside these ranges and needn't reach their ends.
Inputs may be any that keep to these rules, and one draw needn't show every extreme that they name: `left_sector`: among the 64 blocks of one wave index no left sector appears more than 2 times, and some sector appears exactly 2 times. `sector_owner`: each wave index holds the environments of exactly one sector.
All inputs are finite; a program needn't handle non-finite values.
Results may differ from the reference program's by a relative error of at most 0.013.
Values may be sent and summed in bfloat16 or wider, within the bound.
A program may use at most 128 MiB of HBM per device.

```python
import math
import jax
import jax.numpy as jnp
import numpy as np
from jax import lax

BLK = 128
CH = 40
PSI_DEV = 64
SECTORS = 64
CAP = 2
BLOCKS = 4096
N_ENV = 4


def with_ends(drawn, rng, least, top_value):
    spot = [jax.random.randint(jax.random.fold_in(rng, axis), (), 0, length) for axis, length in enumerate(drawn.shape)]
    main_axis = drawn.shape.index(max(drawn.shape))
    neighbour = spot[:main_axis] + [(spot[main_axis] + 1) % drawn.shape[main_axis]] + spot[main_axis + 1:]
    return drawn.at[tuple(spot)].set(least).at[tuple(neighbour)].set(top_value)


def level_of(rng, shape, cuts, least, high):
    def one(dim, shards_of):
        draws = jax.random.uniform(jax.random.fold_in(jax.random.fold_in(rng, 6), dim), (shards_of,), jnp.float32, least / len(cuts), high / len(cuts))
        return jnp.repeat(jnp.exp(draws), shape[dim] // shards_of).reshape((-1,) + (1,) * (len(shape) - dim - 1))

    gain = one(*cuts[0])
    for cut in cuts[1:]:
        gain = gain * one(*cut)
    return gain


def assign_block(rng, own, number, rows, amount, top, limit, slope):
    order = jax.random.permutation(rng, amount)
    crowded, usual = shares(amount, rows * top, limit, slope, True), shares(amount, rows * top, limit, slope, False)
    places = jnp.arange(amount)

    def named(sizes, turn):
        used = int((sizes > 0).sum())
        fixed = max(1, used // 4)
        passed = fixed + (places - fixed + turn * (used - fixed)) % max(1, amount - fixed)
        return jnp.zeros((amount,), jnp.int32).at[order[jnp.where(places < fixed, places, passed)]].set(jnp.asarray(sizes, jnp.int32))

    sizes = jnp.where(number % 4 == 0, named(crowded, number // 4), named(usual, number - number // 4 - 1))
    mixed = jax.random.permutation(jax.random.fold_in(own, 3), amount)
    donor, taker = mixed[0:amount // 2 * 2:2], mixed[1:amount // 2 * 2:2]
    room = jnp.minimum(sizes[donor] - 1, limit - sizes[taker]) // 2
    room = jnp.where((donor == order[0]) | (taker == order[0]) | (sizes[taker] == 0), 0, jnp.maximum(room, 0))
    passed = jax.random.randint(jax.random.fold_in(own, 4), (amount // 2,), 0, 1 << 20) % (room + 1)
    sizes = sizes.at[donor].add(-passed).at[taker].add(passed)
    items = jnp.searchsorted(jnp.cumsum(sizes), jnp.arange(rows * top), side="right").astype(jnp.int32)
    table = items.reshape(top, rows).T
    table = table[jax.random.permutation(jax.random.fold_in(own, 1), rows)]
    turn = jax.random.randint(jax.random.fold_in(own, 2), (rows, 1), 0, top)
    return jnp.take_along_axis(table, (jnp.arange(top)[None, :] + turn) % top, axis=1)


def shares(amount, total, bound, slope, full):
    weights = [(1 << 20) // math.isqrt(rank ** slope) + 1 for rank in range(1, amount + 1)]
    largest = bound if full else min(bound, max(-(-total // amount), total * weights[0] // sum(weights)))
    least = 1 if total - largest >= amount - 1 else 0
    given, rest = [largest] + [least] * (amount - 1), total - largest - least * (amount - 1)
    while rest > 0:
        candidates = [i for i in range(1, amount) if given[i] < largest] or [i for i in range(1, amount) if given[i] < bound]
        mass, left = sum([weights[i] for i in candidates]), rest
        for i in candidates:
            extra = min(bound - given[i], max(1, left * weights[i] // mass), rest)
            given[i] = given[i] + extra
            rest = rest - extra
    return np.array(given)


def bell_draw(stream_key, dims, spread, most, pieces=(), kind=jnp.bfloat16):
    entries = jax.random.normal(stream_key, dims, jnp.float32) * spread
    if len(pieces) > 0:
        entries = level_of(stream_key, dims, pieces, -0.22, 0.18) * entries
    return jnp.clip(entries, min=-most, max=most).astype(kind)


def setup_inputs(seed: int = 0) -> dict:
    arg_keys = jax.random.split(jax.random.key(seed), 8)
    psi = bell_draw(arg_keys[0], (BLOCKS, BLK, BLK), 1.0, 6.0, ((0, 64),))
    left_env = bell_draw(arg_keys[1], (CH, SECTORS, BLK, BLK), BLK ** -0.5, 0.5, ((0, 4), (1, 64)))
    right_env = bell_draw(arg_keys[2], (CH, SECTORS, BLK, BLK), (BLK * CH) ** -0.5, 0.078125, ((0, 4), (1, 64)))
    left_sector_keys = jax.random.split(jax.random.fold_in(arg_keys[3], 1), BLOCKS // PSI_DEV)
    left_sector_turns = jax.random.permutation(jax.random.fold_in(arg_keys[3], 3), BLOCKS // PSI_DEV)
    left_sector = jax.vmap(lambda own, number: assign_block(jax.random.fold_in(arg_keys[3], 2), own, number, PSI_DEV, SECTORS, 1, CAP, 2))(left_sector_keys, left_sector_turns).reshape((BLOCKS, 1))
    right_sector = with_ends(jax.random.randint(arg_keys[4], (BLOCKS, 1), 0, SECTORS), jax.random.fold_in(arg_keys[4], 1), 0, SECTORS - 1).astype(jnp.int32)
    sector_owner = jax.random.permutation(arg_keys[5], SECTORS).astype(jnp.int32)
    sector_rows = with_ends(jax.random.randint(arg_keys[6], (SECTORS,), BLK // 2, BLK + 1), jax.random.fold_in(arg_keys[6], 1), BLK // 2, BLK).astype(jnp.int32)
    return {"psi": psi, "left_env": left_env, "right_env": right_env, "left_sector": left_sector, "right_sector": right_sector, "sector_owner": sector_owner, "sector_rows": sector_rows}


def reference(psi, left_env, right_env, left_sector, right_sector, sector_owner, sector_rows):
    group = CH // N_ENV
    lsec = left_sector[:, 0].astype(jnp.int32)
    rsec = right_sector[:, 0].astype(jnp.int32)
    lpos = sector_owner[lsec].astype(jnp.int32)
    rpos = sector_owner[rsec].astype(jnp.int32)
    lrows = sector_rows[lsec].astype(jnp.int32)
    rrows = sector_rows[rsec].astype(jnp.int32)
    line = jnp.arange(BLK, dtype=jnp.int32)

    def one_block(items):
        block, lplace, rplace, lcount, rcount = items
        mask = (line[:, None] < lcount) & (line[None, :] < rcount)
        masked = jnp.where(mask, block, jnp.zeros_like(block))
        lmats = jnp.take(left_env, lplace, axis=1)
        rmats = jnp.take(right_env, rplace, axis=1)
        inner = jnp.einsum("wab,bc->wac", lmats.astype(jnp.float32), masked.astype(jnp.float32))
        inner = inner.astype(jnp.bfloat16)
        terms = jnp.einsum("wac,wcd->wad", inner.astype(jnp.float32), rmats.astype(jnp.float32))
        parts = jnp.sum(terms.reshape(N_ENV, group, BLK, BLK), axis=1).astype(jnp.bfloat16)
        total = jnp.sum(parts.astype(jnp.float32), axis=0)
        return jnp.where(mask, total, jnp.zeros_like(total)).astype(jnp.bfloat16)

    return lax.map(one_block, (psi, lpos, rpos, lrows, rrows))
```

```python
import functools

import jax
import jax.numpy as jnp
from jax import lax
from jax.experimental import pallas as pl
from jax.experimental.pallas import tpu as pltpu
from jax.sharding import PartitionSpec as P


def block_kernel(lpos, rpos, lrows, rrows, psi_ref, l_ref, r_ref, out_ref):
    k = pl.program_id(0)
    width = psi_ref.shape[1]
    rows = lax.broadcasted_iota(jnp.int32, (width, width), 0)
    cols = lax.broadcasted_iota(jnp.int32, (width, width), 1)
    mask = (rows < lrows[k]) & (cols < rrows[k])
    masked = jnp.where(mask, psi_ref[0], jnp.zeros_like(psi_ref[0]))
    acc = jnp.zeros((width, width), jnp.float32)
    for w in range(l_ref.shape[0]):
        y = jnp.dot(l_ref[w, 0], masked, preferred_element_type=jnp.float32)
        acc = acc + jnp.dot(y.astype(jnp.bfloat16), r_ref[w, 0], preferred_element_type=jnp.float32)
    out_ref[0] = jnp.where(mask, acc, 0.0).astype(out_ref.dtype)


def apply_blocks(psi, left_all, right_all, lpos, rpos, lrows, rrows):
    count, width, _ = psi.shape
    chans = left_all.shape[0]
    grid_spec = pltpu.PrefetchScalarGridSpec(
        num_scalar_prefetch=4,
        grid=(count,),
        in_specs=[
            pl.BlockSpec((1, width, width), lambda k, lp, rp, lr, rr: (k, 0, 0)),
            pl.BlockSpec((chans, 1, width, width), lambda k, lp, rp, lr, rr: (0, lp[k], 0, 0)),
            pl.BlockSpec((chans, 1, width, width), lambda k, lp, rp, lr, rr: (0, rp[k], 0, 0)),
        ],
        out_specs=pl.BlockSpec((1, width, width), lambda k, lp, rp, lr, rr: (k, 0, 0)),
    )
    flops = count * chans * 4 * width ** 3
    nbytes = count * (2 * chans + 2) * width * width * 2
    return pl.pallas_call(
        block_kernel,
        grid_spec=grid_spec,
        out_shape=jax.ShapeDtypeStruct((count, width, width), jnp.bfloat16),
        cost_estimate=pl.CostEstimate(flops=flops, bytes_accessed=nbytes, transcendentals=0),
    )(lpos, rpos, lrows, rrows, psi, left_all, right_all)


def on_device(psi, left_env, right_env, left_sector, right_sector, sector_owner, sector_rows):
    nenv = lax.axis_size("env")
    count, width, _ = psi.shape
    lsec = left_sector[:, 0]
    rsec = right_sector[:, 0]
    lpos = sector_owner[lsec]
    rpos = sector_owner[rsec]
    lrows = sector_rows[lsec]
    rrows = sector_rows[rsec]
    left_all = lax.all_gather(left_env, "wave", axis=1, tiled=True)
    right_all = lax.all_gather(right_env, "wave", axis=1, tiled=True)
    part = apply_blocks(psi, left_all, right_all, lpos, rpos, lrows, rrows)
    share = width // nenv
    part = part.reshape(count, nenv, share, width)
    got = lax.all_to_all(part, "env", split_axis=1, concat_axis=1, tiled=True)
    total = jnp.sum(got.astype(jnp.float32), axis=1)
    return total.astype(jnp.bfloat16)


def solution(mesh):
    return jax.shard_map(
        on_device,
        mesh=mesh,
        in_specs=(
            P("wave", None, None),
            P("env", "wave", None, None),
            P("env", "wave", None, None),
            P("wave", None),
            P("wave", None),
            P(),
            P(),
        ),
        out_specs=P("wave", "env", None),
        check_vma=False,
    )
```

```python
import functools

import jax
import jax.numpy as jnp
from jax import lax
from jax.experimental import pallas as pl
from jax.experimental.pallas import tpu as pltpu
from jax.sharding import PartitionSpec as P


def block_kernel(lpos, rpos, lrows, rrows, psi_ref, l_ref, r_ref, out_ref):
    k = pl.program_id(0)
    width = psi_ref.shape[1]
    rows = lax.broadcasted_iota(jnp.int32, (width, width), 0)
    cols = lax.broadcasted_iota(jnp.int32, (width, width), 1)
    mask = (rows < lrows[k]) & (cols < rrows[k])
    masked = jnp.where(mask, psi_ref[0], jnp.zeros_like(psi_ref[0]))
    chans = l_ref.shape[0]
    lmat = l_ref[...].reshape(chans * width, width)
    y = jnp.dot(lmat, masked, preferred_element_type=jnp.float32).astype(jnp.bfloat16)
    ywide = jnp.concatenate([y[w * width:(w + 1) * width] for w in range(chans)], axis=1)
    rmat = r_ref[...].reshape(chans * width, width)
    acc = jnp.dot(ywide, rmat, preferred_element_type=jnp.float32)
    out_ref[0] = jnp.where(mask, acc, 0.0).astype(out_ref.dtype)


def apply_blocks(psi, left_all, right_all, lpos, rpos, lrows, rrows):
    count, width, _ = psi.shape
    chans = left_all.shape[0]
    grid_spec = pltpu.PrefetchScalarGridSpec(
        num_scalar_prefetch=4,
        grid=(count,),
        in_specs=[
            pl.BlockSpec((1, width, width), lambda k, lp, rp, lr, rr: (k, 0, 0)),
            pl.BlockSpec((chans, 1, width, width), lambda k, lp, rp, lr, rr: (0, lp[k], 0, 0)),
            pl.BlockSpec((chans, 1, width, width), lambda k, lp, rp, lr, rr: (0, rp[k], 0, 0)),
        ],
        out_specs=pl.BlockSpec((1, width, width), lambda k, lp, rp, lr, rr: (k, 0, 0)),
    )
    flops = count * chans * 4 * width ** 3
    nbytes = count * (2 * chans + 2) * width * width * 2
    return pl.pallas_call(
        block_kernel,
        grid_spec=grid_spec,
        out_shape=jax.ShapeDtypeStruct((count, width, width), jnp.bfloat16),
        cost_estimate=pl.CostEstimate(flops=flops, bytes_accessed=nbytes, transcendentals=0),
    )(lpos, rpos, lrows, rrows, psi, left_all, right_all)


def gather_env(env):
    chans, _, width, _ = env.shape
    over_chips = lax.all_gather(env, "chip", axis=1, tiled=True)
    both = lax.all_gather(over_chips, "core", axis=2)
    return both.reshape(chans, -1, width, width)


def on_device(psi, left_env, right_env, left_sector, right_sector, sector_owner, sector_rows):
    nenv = lax.axis_size("env")
    count, width, _ = psi.shape
    lsec = left_sector[:, 0]
    rsec = right_sector[:, 0]
    lpos = sector_owner[lsec]
    rpos = sector_owner[rsec]
    lrows = sector_rows[lsec]
    rrows = sector_rows[rsec]
    left_all = gather_env(left_env)
    right_all = gather_env(right_env)
    part = apply_blocks(psi, left_all, right_all, lpos, rpos, lrows, rrows)
    share = width // nenv
    part = part.reshape(count, nenv, share, width)
    got = lax.all_to_all(part, "env", split_axis=1, concat_axis=1, tiled=True)
    total = jnp.sum(got.astype(jnp.float32), axis=1)
    return total.astype(jnp.bfloat16)


def solution(mesh):
    nenv, nwave = mesh.devices.shape
    split = jax.sharding.Mesh(mesh.devices.reshape(nenv, nwave // 2, 2), ("env", "chip", "core"))
    wave = ("chip", "core")
    return jax.shard_map(
        on_device,
        mesh=split,
        in_specs=(
            P(wave, None, None),
            P("env", wave, None, None),
            P("env", wave, None, None),
            P(wave, None),
            P(wave, None),
            P(),
            P(),
        ),
        out_specs=P(wave, "env", None),
        check_vma=False,
    )
```

```python
import functools

import jax
import jax.numpy as jnp
from jax import lax
from jax.experimental import pallas as pl
from jax.experimental.pallas import tpu as pltpu
from jax.sharding import PartitionSpec as P

MESH = pl.DeviceIdType.MESH
NY, NZ = 4, 8


def gather_kernel(x_ref, g_ref, own_sem, recv, sent):
    e = lax.axis_index("env")
    y = lax.axis_index("y")
    z = lax.axis_index("z")
    c = lax.axis_index("core")

    def dev(yy, zz, cc):
        return (e, lax.rem(yy + NY, NY), lax.rem(zz + NZ, NZ), cc)

    def slot(yy, zz, cc):
        return (lax.rem(yy + NY, NY) * NZ + lax.rem(zz + NZ, NZ)) * 2 + cc

    barrier = pltpu.get_barrier_semaphore()
    peers = [dev(y + 1, z, c), dev(y - 1, z, c), dev(y, z + 1, c), dev(y, z - 1, c), dev(y, z, 1 - c)]
    for p in peers:
        pl.semaphore_signal(barrier, inc=1, device_id=p, device_id_type=MESH)
    pl.semaphore_wait(barrier, len(peers))

    own = pltpu.make_async_copy(x_ref, g_ref.at[slot(y, z, c)], own_sem)
    own.start()

    def role(cc, first, second):
        fsize, fstep = first
        ssize, sstep = second
        fplus, fminus = fsize // 2, fsize - 1 - fsize // 2
        splus, sminus = ssize // 2, ssize - 1 - ssize // 2
        sends = []

        def origin(a, b):
            fy, fz = fstep(a)
            sy, sz = sstep(b)
            return y - fy - sy, z - fz - sz

        def send(src, a, b, target, kind):
            oy, oz = origin(a, b)
            s = slot(oy, oz, cc)
            cp = pltpu.make_async_remote_copy(
                src_ref=src, dst_ref=g_ref.at[s], send_sem=sent.at[s, kind],
                recv_sem=recv.at[s], device_id=target, device_id_type=MESH)
            cp.start()
            sends.append(cp)

        def wait_in(a, b):
            oy, oz = origin(a, b)
            s = slot(oy, oz, cc)
            cp = pltpu.make_async_remote_copy(
                src_ref=g_ref.at[s], dst_ref=g_ref.at[s], send_sem=sent.at[s, 0],
                recv_sem=recv.at[s], device_id=dev(y, z, 1 - cc), device_id_type=MESH)
            cp.wait_recv()

        def held(a, b):
            oy, oz = origin(a, b)
            return g_ref.at[slot(oy, oz, cc)]

        fp_y, fp_z = fstep(1)
        sp_y, sp_z = sstep(1)
        f_next, f_prev = dev(y + fp_y, z + fp_z, cc), dev(y - fp_y, z - fp_z, cc)
        s_next, s_prev = dev(y + sp_y, z + sp_z, cc), dev(y - sp_y, z - sp_z, cc)
        partner = dev(y, z, 1 - cc)

        def spread(src, a, b):
            if b == 0:
                send(src, a, 0, s_next, 2)
                send(src, a, 0, s_prev, 3)
            elif 0 < b < splus:
                send(src, a, b, s_next, 2)
            elif 0 < -b < sminus:
                send(src, a, b, s_prev, 3)
            send(src, a, b, partner, 4)

        send(x_ref, 0, 0, f_next, 0)
        send(x_ref, 0, 0, f_prev, 1)
        spread(x_ref, 0, 0)
        for step in range(1, max(fplus, fminus) + 1):
            for a in (step, -step):
                if (a > 0 and a > fplus) or (a < 0 and -a > fminus):
                    continue
                wait_in(a, 0)
                if 0 < a < fplus:
                    send(held(a, 0), a, 0, f_next, 0)
                if 0 < -a < fminus:
                    send(held(a, 0), a, 0, f_prev, 1)
                spread(held(a, 0), a, 0)
        row = list(range(-fminus, fplus + 1))
        for step in range(1, max(splus, sminus) + 1):
            for b in (step, -step):
                if (b > 0 and b > splus) or (b < 0 and -b > sminus):
                    continue
                for a in row:
                    wait_in(a, b)
                    spread(held(a, b), a, b)
        for yy in range(NY):
            for zz in range(NZ):
                s = (yy * NZ + zz) * 2 + (1 - cc)
                cp = pltpu.make_async_remote_copy(
                    src_ref=g_ref.at[s], dst_ref=g_ref.at[s], send_sem=sent.at[s, 0],
                    recv_sem=recv.at[s], device_id=partner, device_id_type=MESH)
                cp.wait_recv()
        for cp in sends:
            cp.wait_send()

    zstep = lambda d: (0, d)
    ystep = lambda d: (d, 0)

    @pl.when(c == 0)
    def _():
        role(0, (NZ, zstep), (NY, ystep))

    @pl.when(c == 1)
    def _():
        role(1, (NY, ystep), (NZ, zstep))

    own.wait()


def gather_env(x):
    shape = (NY * NZ * 2,) + x.shape
    return pl.pallas_call(
        gather_kernel,
        out_shape=jax.ShapeDtypeStruct(shape, x.dtype),
        in_specs=[pl.BlockSpec(memory_space=pl.ANY)],
        out_specs=pl.BlockSpec(memory_space=pl.ANY),
        scratch_shapes=[
            pltpu.SemaphoreType.DMA(()),
            pltpu.SemaphoreType.DMA((NY * NZ * 2,)),
            pltpu.SemaphoreType.DMA((NY * NZ * 2, 5)),
        ],
        compiler_params=pltpu.CompilerParams(collective_id=0, has_side_effects=True),
    )(x)


def block_kernel(lpos, rpos, lrows, rrows, psi_ref, l_ref, r_ref, out_ref):
    k = pl.program_id(0)
    width = psi_ref.shape[1]
    rows = lax.broadcasted_iota(jnp.int32, (width, width), 0)
    cols = lax.broadcasted_iota(jnp.int32, (width, width), 1)
    mask = (rows < lrows[k]) & (cols < rrows[k])
    masked = jnp.where(mask, psi_ref[0], jnp.zeros_like(psi_ref[0]))
    chans = l_ref.shape[1]
    lmat = l_ref[...].reshape(chans * width, width)
    y = jnp.dot(lmat, masked, preferred_element_type=jnp.float32).astype(jnp.bfloat16)
    ywide = jnp.concatenate([y[w * width:(w + 1) * width] for w in range(chans)], axis=1)
    rmat = r_ref[...].reshape(chans * width, width)
    acc = jnp.dot(ywide, rmat, preferred_element_type=jnp.float32)
    out_ref[0] = jnp.where(mask, acc, 0.0).astype(out_ref.dtype)


def apply_blocks(psi, both, lpos, rpos, lrows, rrows):
    count, width, _ = psi.shape
    chans = both.shape[1] // 2
    grid_spec = pltpu.PrefetchScalarGridSpec(
        num_scalar_prefetch=4,
        grid=(count,),
        in_specs=[
            pl.BlockSpec((1, width, width), lambda k, lp, rp, lr, rr: (k, 0, 0)),
            pl.BlockSpec((1, chans, width, width), lambda k, lp, rp, lr, rr: (lp[k], 0, 0, 0)),
            pl.BlockSpec((1, chans, width, width), lambda k, lp, rp, lr, rr: (rp[k], 1, 0, 0)),
        ],
        out_specs=pl.BlockSpec((1, width, width), lambda k, lp, rp, lr, rr: (k, 0, 0)),
    )
    flops = count * chans * 4 * width ** 3
    nbytes = count * (2 * chans + 2) * width * width * 2
    return pl.pallas_call(
        block_kernel,
        grid_spec=grid_spec,
        out_shape=jax.ShapeDtypeStruct((count, width, width), jnp.bfloat16),
        cost_estimate=pl.CostEstimate(flops=flops, bytes_accessed=nbytes, transcendentals=0),
    )(lpos, rpos, lrows, rrows, psi, both, both)


def on_device(psi, left_env, right_env, left_sector, right_sector, sector_owner, sector_rows):
    nenv = lax.axis_size("env")
    count, width, _ = psi.shape
    lsec = left_sector[:, 0]
    rsec = right_sector[:, 0]
    lpos = sector_owner[lsec]
    rpos = sector_owner[rsec]
    lrows = sector_rows[lsec]
    rrows = sector_rows[rsec]
    both = gather_env(jnp.concatenate([left_env[:, 0], right_env[:, 0]], axis=0))
    part = apply_blocks(psi, both, lpos, rpos, lrows, rrows)
    share = width // nenv
    part = part.reshape(count, nenv, share, width)
    got = lax.all_to_all(part, "env", split_axis=1, concat_axis=1, tiled=True)
    total = jnp.sum(got.astype(jnp.float32), axis=1)
    return total.astype(jnp.bfloat16)


def solution(mesh):
    nenv, nwave = mesh.devices.shape
    split = jax.sharding.Mesh(mesh.devices.reshape(nenv, NY, NZ, 2), ("env", "y", "z", "core"))
    wave = ("y", "z", "core")
    return jax.shard_map(
        on_device,
        mesh=split,
        in_specs=(
            P(wave, None, None),
            P("env", wave, None, None),
            P("env", wave, None, None),
            P(wave, None),
            P(wave, None),
            P(),
            P(),
        ),
        out_specs=P(wave, "env", None),
        check_vma=False,
    )
```

```python
import functools

import jax
import jax.numpy as jnp
from jax import lax
from jax.experimental import pallas as pl
from jax.experimental.pallas import tpu as pltpu
from jax.sharding import PartitionSpec as P

MESH = pl.DeviceIdType.MESH
NY, NZ = 4, 8


def gather_kernel(x_ref, g_ref, own_sem, recv, sent):
    e = lax.axis_index("env")
    y = lax.axis_index("y")
    z = lax.axis_index("z")
    c = lax.axis_index("core")

    def dev(yy, zz, cc):
        return (e, lax.rem(yy + NY, NY), lax.rem(zz + NZ, NZ), cc)

    def slot(yy, zz, cc):
        return (lax.rem(yy + NY, NY) * NZ + lax.rem(zz + NZ, NZ)) * 2 + cc

    barrier = pltpu.get_barrier_semaphore()
    peers = [dev(y + 1, z, c), dev(y - 1, z, c), dev(y, z + 1, c), dev(y, z - 1, c), dev(y, z, 1 - c)]
    for p in peers:
        pl.semaphore_signal(barrier, inc=1, device_id=p, device_id_type=MESH)
    pl.semaphore_wait(barrier, len(peers))

    own = pltpu.make_async_copy(x_ref, g_ref.at[slot(y, z, c)], own_sem)
    own.start()

    def role(cc, first, second):
        fsize, fstep = first
        ssize, sstep = second
        fplus, fminus = fsize // 2, fsize - 1 - fsize // 2
        splus, sminus = ssize // 2, ssize - 1 - ssize // 2
        sends = []

        def origin(a, b):
            fy, fz = fstep(a)
            sy, sz = sstep(b)
            return y - fy - sy, z - fz - sz

        def send(src, a, b, target, kind):
            oy, oz = origin(a, b)
            s = slot(oy, oz, cc)
            cp = pltpu.make_async_remote_copy(
                src_ref=src, dst_ref=g_ref.at[s], send_sem=sent.at[s, kind],
                recv_sem=recv.at[s], device_id=target, device_id_type=MESH)
            cp.start()
            sends.append(cp)

        def wait_in(a, b):
            oy, oz = origin(a, b)
            s = slot(oy, oz, cc)
            cp = pltpu.make_async_remote_copy(
                src_ref=g_ref.at[s], dst_ref=g_ref.at[s], send_sem=sent.at[s, 0],
                recv_sem=recv.at[s], device_id=dev(y, z, 1 - cc), device_id_type=MESH)
            cp.wait_recv()

        def held(a, b):
            oy, oz = origin(a, b)
            return g_ref.at[slot(oy, oz, cc)]

        fp_y, fp_z = fstep(1)
        sp_y, sp_z = sstep(1)
        f_next, f_prev = dev(y + fp_y, z + fp_z, cc), dev(y - fp_y, z - fp_z, cc)
        s_next, s_prev = dev(y + sp_y, z + sp_z, cc), dev(y - sp_y, z - sp_z, cc)
        partner = dev(y, z, 1 - cc)

        def spread(src, a, b):
            if b == 0:
                send(src, a, 0, s_next, 2)
                send(src, a, 0, s_prev, 3)
            elif 0 < b < splus:
                send(src, a, b, s_next, 2)
            elif 0 < -b < sminus:
                send(src, a, b, s_prev, 3)
            send(src, a, b, partner, 4)

        send(x_ref, 0, 0, f_next, 0)
        send(x_ref, 0, 0, f_prev, 1)
        spread(x_ref, 0, 0)
        for step in range(1, max(fplus, fminus) + 1):
            for a in (step, -step):
                if (a > 0 and a > fplus) or (a < 0 and -a > fminus):
                    continue
                wait_in(a, 0)
                if 0 < a < fplus:
                    send(held(a, 0), a, 0, f_next, 0)
                if 0 < -a < fminus:
                    send(held(a, 0), a, 0, f_prev, 1)
                spread(held(a, 0), a, 0)
        row = list(range(-fminus, fplus + 1))
        for step in range(1, max(splus, sminus) + 1):
            for b in (step, -step):
                if (b > 0 and b > splus) or (b < 0 and -b > sminus):
                    continue
                for a in row:
                    wait_in(a, b)
                    spread(held(a, b), a, b)
        for yy in range(NY):
            for zz in range(NZ):
                s = (yy * NZ + zz) * 2 + (1 - cc)
                cp = pltpu.make_async_remote_copy(
                    src_ref=g_ref.at[s], dst_ref=g_ref.at[s], send_sem=sent.at[s, 0],
                    recv_sem=recv.at[s], device_id=partner, device_id_type=MESH)
                cp.wait_recv()
        for cp in sends:
            cp.wait_send()

    zstep = lambda d: (0, d)
    ystep = lambda d: (d, 0)

    @pl.when(c == 0)
    def _():
        role(0, (NZ, zstep), (NY, ystep))

    @pl.when(c == 1)
    def _():
        role(1, (NY, ystep), (NZ, zstep))

    own.wait()


def gather_env(x):
    shape = (NY * NZ * 2,) + x.shape
    return pl.pallas_call(
        gather_kernel,
        out_shape=jax.ShapeDtypeStruct(shape, x.dtype),
        in_specs=[pl.BlockSpec(memory_space=pl.ANY)],
        out_specs=pl.BlockSpec(memory_space=pl.ANY),
        scratch_shapes=[
            pltpu.SemaphoreType.DMA(()),
            pltpu.SemaphoreType.DMA((NY * NZ * 2,)),
            pltpu.SemaphoreType.DMA((NY * NZ * 2, 5)),
        ],
        compiler_params=pltpu.CompilerParams(collective_id=0, has_side_effects=True),
    )(x)


def block_kernel(base, lsec, rsec, owner, live, psi_ref, l_ref, r_ref, out_ref):
    k = pl.program_id(0) + base
    width = psi_ref.shape[1]
    rows = lax.broadcasted_iota(jnp.int32, (width, width), 0)
    cols = lax.broadcasted_iota(jnp.int32, (width, width), 1)
    mask = (rows < live[lsec[k]]) & (cols < live[rsec[k]])
    masked = jnp.where(mask, psi_ref[0], jnp.zeros_like(psi_ref[0]))
    chans = l_ref.shape[1]
    lmat = l_ref[...].reshape(chans * width, width)
    y = jnp.dot(lmat, masked, preferred_element_type=jnp.float32).astype(jnp.bfloat16)
    ywide = jnp.concatenate([y[w * width:(w + 1) * width] for w in range(chans)], axis=1)
    rmat = r_ref[...].reshape(chans * width, width)
    acc = jnp.dot(ywide, rmat, preferred_element_type=jnp.float32)
    part = jnp.where(mask, acc, 0.0).astype(jnp.bfloat16)
    out_ref[0] = part.astype(out_ref.dtype)


def apply_blocks(psi, both, lsec, rsec, owner, live, base, size):
    count, width, _ = psi.shape
    chans = both.shape[1] // 2
    grid_spec = pltpu.PrefetchScalarGridSpec(
        num_scalar_prefetch=4,
        grid=(size,),
        in_specs=[
            pl.BlockSpec((1, width, width), lambda k, ls, rs, ow, lv: (k + base, 0, 0)),
            pl.BlockSpec((1, chans, width, width), lambda k, ls, rs, ow, lv: (ow[ls[k + base]], 0, 0, 0)),
            pl.BlockSpec((1, chans, width, width), lambda k, ls, rs, ow, lv: (ow[rs[k + base]], 1, 0, 0)),
        ],
        out_specs=pl.BlockSpec((1, width, width), lambda k, ls, rs, ow, lv: (k, 0, 0)),
    )
    flops = size * chans * 4 * width ** 3
    nbytes = size * (2 * chans + 3) * width * width * 2
    return pl.pallas_call(
        functools.partial(block_kernel, base),
        grid_spec=grid_spec,
        out_shape=jax.ShapeDtypeStruct((size, width, width), jnp.float32),
        cost_estimate=pl.CostEstimate(flops=flops, bytes_accessed=nbytes, transcendentals=0),
    )(lsec, rsec, owner, live, psi, both, both)


def on_device(psi, left_env, right_env, left_sector, right_sector, sector_owner, sector_rows):
    count, width, _ = psi.shape
    lsec = left_sector[:, 0]
    rsec = right_sector[:, 0]
    both = gather_env(jnp.concatenate([left_env[:, 0], right_env[:, 0]], axis=0))
    pieces = 4
    size = count // pieces
    outs = []
    for i in range(pieces):
        part = apply_blocks(psi, both, lsec, rsec, sector_owner, sector_rows, i * size, size)
        total = lax.psum_scatter(part, "env", scatter_dimension=1, tiled=True)
        outs.append(total.astype(jnp.bfloat16))
    return jnp.concatenate(outs, axis=0)


def solution(mesh):
    nenv, nwave = mesh.devices.shape
    split = jax.sharding.Mesh(mesh.devices.reshape(nenv, NY, NZ, 2), ("env", "y", "z", "core"))
    wave = ("y", "z", "core")
    return jax.shard_map(
        on_device,
        mesh=split,
        in_specs=(
            P(wave, None, None),
            P("env", wave, None, None),
            P("env", wave, None, None),
            P(wave, None),
            P(wave, None),
            P(),
            P(),
        ),
        out_specs=P(wave, "env", None),
        check_vma=False,
    )
```

```python
import functools

import jax
import jax.numpy as jnp
from jax import lax
from jax.experimental import pallas as pl
from jax.experimental.pallas import tpu as pltpu
from jax.sharding import PartitionSpec as P

MESH = pl.DeviceIdType.MESH
NY, NZ = 4, 8


def gather_kernel(x_ref, g_ref, own_sem, recv, sent):
    e = lax.axis_index("env")
    y = lax.axis_index("y")
    z = lax.axis_index("z")
    c = lax.axis_index("core")

    def dev(yy, zz, cc):
        return (e, lax.rem(yy + NY, NY), lax.rem(zz + NZ, NZ), cc)

    def slot(yy, zz, cc):
        return (lax.rem(yy + NY, NY) * NZ + lax.rem(zz + NZ, NZ)) * 2 + cc

    barrier = pltpu.get_barrier_semaphore()
    peers = [dev(y + 1, z, c), dev(y - 1, z, c), dev(y, z + 1, c), dev(y, z - 1, c), dev(y, z, 1 - c)]
    for p in peers:
        pl.semaphore_signal(barrier, inc=1, device_id=p, device_id_type=MESH)
    pl.semaphore_wait(barrier, len(peers))

    own = pltpu.make_async_copy(x_ref, g_ref.at[slot(y, z, c)], own_sem)
    own.start()

    def role(cc, first, second):
        fsize, fstep = first
        ssize, sstep = second
        fplus, fminus = fsize // 2, fsize - 1 - fsize // 2
        splus, sminus = ssize // 2, ssize - 1 - ssize // 2
        sends = []

        def origin(a, b):
            fy, fz = fstep(a)
            sy, sz = sstep(b)
            return y - fy - sy, z - fz - sz

        def send(src, a, b, target, kind):
            oy, oz = origin(a, b)
            s = slot(oy, oz, cc)
            cp = pltpu.make_async_remote_copy(
                src_ref=src, dst_ref=g_ref.at[s], send_sem=sent.at[s, kind],
                recv_sem=recv.at[s], device_id=target, device_id_type=MESH)
            cp.start()
            sends.append(cp)

        def wait_in(a, b):
            oy, oz = origin(a, b)
            s = slot(oy, oz, cc)
            cp = pltpu.make_async_remote_copy(
                src_ref=g_ref.at[s], dst_ref=g_ref.at[s], send_sem=sent.at[s, 0],
                recv_sem=recv.at[s], device_id=dev(y, z, 1 - cc), device_id_type=MESH)
            cp.wait_recv()

        def held(a, b):
            oy, oz = origin(a, b)
            return g_ref.at[slot(oy, oz, cc)]

        fp_y, fp_z = fstep(1)
        sp_y, sp_z = sstep(1)
        f_next, f_prev = dev(y + fp_y, z + fp_z, cc), dev(y - fp_y, z - fp_z, cc)
        s_next, s_prev = dev(y + sp_y, z + sp_z, cc), dev(y - sp_y, z - sp_z, cc)
        partner = dev(y, z, 1 - cc)

        def spread(src, a, b):
            if b == 0:
                send(src, a, 0, s_next, 2)
                send(src, a, 0, s_prev, 3)
            elif 0 < b < splus:
                send(src, a, b, s_next, 2)
            elif 0 < -b < sminus:
                send(src, a, b, s_prev, 3)
            send(src, a, b, partner, 4)

        send(x_ref, 0, 0, f_next, 0)
        send(x_ref, 0, 0, f_prev, 1)
        spread(x_ref, 0, 0)
        for step in range(1, max(fplus, fminus) + 1):
            for a in (step, -step):
                if (a > 0 and a > fplus) or (a < 0 and -a > fminus):
                    continue
                wait_in(a, 0)
                if 0 < a < fplus:
                    send(held(a, 0), a, 0, f_next, 0)
                if 0 < -a < fminus:
                    send(held(a, 0), a, 0, f_prev, 1)
                spread(held(a, 0), a, 0)
        row = list(range(-fminus, fplus + 1))
        for step in range(1, max(splus, sminus) + 1):
            for b in (step, -step):
                if (b > 0 and b > splus) or (b < 0 and -b > sminus):
                    continue
                for a in row:
                    wait_in(a, b)
                    spread(held(a, b), a, b)
        for yy in range(NY):
            for zz in range(NZ):
                s = (yy * NZ + zz) * 2 + (1 - cc)
                cp = pltpu.make_async_remote_copy(
                    src_ref=g_ref.at[s], dst_ref=g_ref.at[s], send_sem=sent.at[s, 0],
                    recv_sem=recv.at[s], device_id=partner, device_id_type=MESH)
                cp.wait_recv()
        for cp in sends:
            cp.wait_send()

    zstep = lambda d: (0, d)
    ystep = lambda d: (d, 0)

    @pl.when(c == 0)
    def _():
        role(0, (NZ, zstep), (NY, ystep))

    @pl.when(c == 1)
    def _():
        role(1, (NY, ystep), (NZ, zstep))

    own.wait()


def gather_env(x):
    shape = (NY * NZ * 2,) + x.shape
    return pl.pallas_call(
        gather_kernel,
        out_shape=jax.ShapeDtypeStruct(shape, x.dtype),
        in_specs=[pl.BlockSpec(memory_space=pl.ANY)],
        out_specs=pl.BlockSpec(memory_space=pl.ANY),
        scratch_shapes=[
            pltpu.SemaphoreType.DMA(()),
            pltpu.SemaphoreType.DMA((NY * NZ * 2,)),
            pltpu.SemaphoreType.DMA((NY * NZ * 2, 5)),
        ],
        compiler_params=pltpu.CompilerParams(collective_id=0, has_side_effects=True),
    )(x)


def block_kernel(order, lsec, rsec, owner, live, psi_ref, l_ref, r_ref, out_ref):
    k = order[pl.program_id(0)]
    width = psi_ref.shape[1]
    rows = lax.broadcasted_iota(jnp.int32, (width, width), 0)
    cols = lax.broadcasted_iota(jnp.int32, (width, width), 1)
    mask = (rows < live[lsec[k]]) & (cols < live[rsec[k]])
    masked = jnp.where(mask, psi_ref[0], jnp.zeros_like(psi_ref[0]))
    chans = l_ref.shape[1]
    lmat = l_ref[...].reshape(chans * width, width)
    y = jnp.dot(lmat, masked, preferred_element_type=jnp.float32).astype(jnp.bfloat16)
    ywide = jnp.concatenate([y[w * width:(w + 1) * width] for w in range(chans)], axis=1)
    rmat = r_ref[...].reshape(chans * width, width)
    acc = jnp.dot(ywide, rmat, preferred_element_type=jnp.float32)
    out_ref[0] = jnp.where(mask, acc, 0.0).astype(out_ref.dtype)


def apply_blocks(psi, both, order, lsec, rsec, owner, live):
    count, width, _ = psi.shape
    chans = both.shape[1] // 2
    grid_spec = pltpu.PrefetchScalarGridSpec(
        num_scalar_prefetch=5,
        grid=(count,),
        in_specs=[
            pl.BlockSpec((1, width, width), lambda i, od, ls, rs, ow, lv: (od[i], 0, 0)),
            pl.BlockSpec((1, chans, width, width), lambda i, od, ls, rs, ow, lv: (ow[ls[od[i]]], 0, 0, 0)),
            pl.BlockSpec((1, chans, width, width), lambda i, od, ls, rs, ow, lv: (ow[rs[od[i]]], 1, 0, 0)),
        ],
        out_specs=pl.BlockSpec((1, width, width), lambda i, od, ls, rs, ow, lv: (od[i], 0, 0)),
    )
    flops = count * chans * 4 * width ** 3
    nbytes = count * (2 * chans + 2) * width * width * 2
    return pl.pallas_call(
        block_kernel,
        grid_spec=grid_spec,
        out_shape=jax.ShapeDtypeStruct((count, width, width), jnp.bfloat16),
        cost_estimate=pl.CostEstimate(flops=flops, bytes_accessed=nbytes, transcendentals=0),
    )(order, lsec, rsec, owner, live, psi, both, both)


def by_left_sector(lsec):
    count = lsec.shape[0]
    pos = jnp.arange(count, dtype=jnp.int32)
    before = (lsec[None, :] < lsec[:, None]) | ((lsec[None, :] == lsec[:, None]) & (pos[None, :] < pos[:, None]))
    rank = jnp.sum(before.astype(jnp.int32), axis=1)
    return jnp.sum(jnp.where(rank[None, :] == pos[:, None], pos[None, :], 0), axis=1)


def on_device(psi, left_env, right_env, left_sector, right_sector, sector_owner, sector_rows):
    nenv = lax.axis_size("env")
    count, width, _ = psi.shape
    lsec = left_sector[:, 0]
    rsec = right_sector[:, 0]
    order = by_left_sector(lsec)
    both = gather_env(jnp.concatenate([left_env[:, 0], right_env[:, 0]], axis=0))
    part = apply_blocks(psi, both, order, lsec, rsec, sector_owner, sector_rows)
    share = width // nenv
    part = part.reshape(count, nenv, share, width)
    got = lax.all_to_all(part, "env", split_axis=1, concat_axis=1, tiled=True)
    total = jnp.sum(got.astype(jnp.float32), axis=1)
    return total.astype(jnp.bfloat16)


def solution(mesh):
    nenv, nwave = mesh.devices.shape
    split = jax.sharding.Mesh(mesh.devices.reshape(nenv, NY, NZ, 2), ("env", "y", "z", "core"))
    wave = ("y", "z", "core")
    return jax.shard_map(
        on_device,
        mesh=split,
        in_specs=(
            P(wave, None, None),
            P("env", wave, None, None),
            P("env", wave, None, None),
            P(wave, None),
            P(wave, None),
            P(),
            P(),
        ),
        out_specs=P(wave, "env", None),
        check_vma=False,
    )
```

```python
import functools

import jax
import jax.numpy as jnp
from jax import lax
from jax.experimental import pallas as pl
from jax.experimental.pallas import tpu as pltpu
from jax.sharding import PartitionSpec as P

MESH = pl.DeviceIdType.MESH
NY, NZ = 4, 8


def gather_kernel(x_ref, g_ref, own_sem, recv, sent):
    e = lax.axis_index("env")
    y = lax.axis_index("y")
    z = lax.axis_index("z")
    c = lax.axis_index("core")
    half = x_ref.shape[0] // 2

    def dev(yy, zz, cc):
        return (e, lax.rem(yy + 2 * NY, NY), lax.rem(zz + 2 * NZ, NZ), cc)

    def slot(yy, zz, cc):
        return (lax.rem(yy + 2 * NY, NY) * NZ + lax.rem(zz + 2 * NZ, NZ)) * 2 + cc

    barrier = pltpu.get_barrier_semaphore()
    peers = [dev(y + 1, z, c), dev(y - 1, z, c), dev(y, z + 1, c), dev(y, z - 1, c), dev(y, z, 1 - c)]
    for p in peers:
        pl.semaphore_signal(barrier, inc=1, device_id=p, device_id_type=MESH)
    pl.semaphore_wait(barrier, len(peers))

    own = pltpu.make_async_copy(x_ref, g_ref.at[slot(y, z, c)], own_sem)
    own.start()

    def role(cc, first, second):
        fsize, fstep = first
        ssize, sstep = second
        fplus, fminus = fsize // 2, fsize - 1 - fsize // 2
        splus, sminus = ssize // 2, ssize - 1 - ssize // 2
        sends = []
        partner = dev(y, z, 1 - cc)

        def where(a, b, h):
            sign = 1 - 2 * h
            fy, fz = fstep(sign * a)
            sy, sz = sstep(sign * b)
            return y - fy - sy, z - fz - sz

        def part(ref, h):
            return ref.at[pl.ds(h * half, half)]

        def item(a, b, h):
            oy, oz = where(a, b, h)
            return slot(oy, oz, cc)

        def near(h, ring, d):
            sign = 1 - 2 * h
            dy, dz = ring(sign * d)
            return dev(y + dy, z + dz, cc)

        def send(src, a, b, h, target, kind):
            s = item(a, b, h)
            cp = pltpu.make_async_remote_copy(
                src_ref=src, dst_ref=part(g_ref.at[s], h), send_sem=sent.at[s, h, kind],
                recv_sem=recv.at[s, h], device_id=target, device_id_type=MESH)
            cp.start()
            sends.append(cp)

        def wait_in(s, h):
            cp = pltpu.make_async_remote_copy(
                src_ref=part(g_ref.at[s], h), dst_ref=part(g_ref.at[s], h), send_sem=sent.at[s, h, 0],
                recv_sem=recv.at[s, h], device_id=partner, device_id_type=MESH)
            cp.wait_recv()

        def held(a, b, h):
            return part(g_ref.at[item(a, b, h)], h)

        def spread(src, a, b, h):
            if b == 0:
                send(src, a, 0, h, near(h, sstep, 1), 2)
                send(src, a, 0, h, near(h, sstep, -1), 3)
            elif 0 < b < splus:
                send(src, a, b, h, near(h, sstep, 1), 2)
            elif 0 < -b < sminus:
                send(src, a, b, h, near(h, sstep, -1), 3)
            send(src, a, b, h, partner, 4)

        for h in range(2):
            send(part(x_ref, h), 0, 0, h, near(h, fstep, 1), 0)
            send(part(x_ref, h), 0, 0, h, near(h, fstep, -1), 1)
        for h in range(2):
            spread(part(x_ref, h), 0, 0, h)
        for step in range(1, max(fplus, fminus) + 1):
            for a in (step, -step):
                if (a > 0 and a > fplus) or (a < 0 and -a > fminus):
                    continue
                for h in range(2):
                    wait_in(item(a, 0, h), h)
                    if 0 < a < fplus:
                        send(held(a, 0, h), a, 0, h, near(h, fstep, 1), 0)
                    if 0 < -a < fminus:
                        send(held(a, 0, h), a, 0, h, near(h, fstep, -1), 1)
                    spread(held(a, 0, h), a, 0, h)
        row = list(range(-fminus, fplus + 1))
        for step in range(1, max(splus, sminus) + 1):
            for b in (step, -step):
                if (b > 0 and b > splus) or (b < 0 and -b > sminus):
                    continue
                for a in row:
                    for h in range(2):
                        wait_in(item(a, b, h), h)
                        spread(held(a, b, h), a, b, h)
        for yy in range(NY):
            for zz in range(NZ):
                for h in range(2):
                    wait_in((yy * NZ + zz) * 2 + (1 - cc), h)
        for cp in sends:
            cp.wait_send()

    zstep = lambda d: (0, d)
    ystep = lambda d: (d, 0)

    @pl.when(c == 0)
    def _():
        role(0, (NZ, zstep), (NY, ystep))

    @pl.when(c == 1)
    def _():
        role(1, (NY, ystep), (NZ, zstep))

    own.wait()


def gather_env(x):
    shape = (NY * NZ * 2,) + x.shape
    return pl.pallas_call(
        gather_kernel,
        out_shape=jax.ShapeDtypeStruct(shape, x.dtype),
        in_specs=[pl.BlockSpec(memory_space=pl.ANY)],
        out_specs=pl.BlockSpec(memory_space=pl.ANY),
        scratch_shapes=[
            pltpu.SemaphoreType.DMA(()),
            pltpu.SemaphoreType.DMA((NY * NZ * 2, 2)),
            pltpu.SemaphoreType.DMA((NY * NZ * 2, 2, 5)),
        ],
        compiler_params=pltpu.CompilerParams(collective_id=0, has_side_effects=True),
    )(x)


def block_kernel(order, lsec, rsec, owner, live, psi_ref, l_ref, r_ref, out_ref):
    k = order[pl.program_id(0)]
    width = psi_ref.shape[1]
    rows = lax.broadcasted_iota(jnp.int32, (width, width), 0)
    cols = lax.broadcasted_iota(jnp.int32, (width, width), 1)
    mask = (rows < live[lsec[k]]) & (cols < live[rsec[k]])
    masked = jnp.where(mask, psi_ref[0], jnp.zeros_like(psi_ref[0]))
    chans = l_ref.shape[1]
    lmat = l_ref[...].reshape(chans * width, width)
    y = jnp.dot(lmat, masked, preferred_element_type=jnp.float32).astype(jnp.bfloat16)
    ywide = jnp.concatenate([y[w * width:(w + 1) * width] for w in range(chans)], axis=1)
    rmat = r_ref[...].reshape(chans * width, width)
    acc = jnp.dot(ywide, rmat, preferred_element_type=jnp.float32)
    out_ref[0] = jnp.where(mask, acc, 0.0).astype(out_ref.dtype)


def apply_blocks(psi, both, order, lsec, rsec, owner, live):
    count, width, _ = psi.shape
    chans = both.shape[1] // 2
    grid_spec = pltpu.PrefetchScalarGridSpec(
        num_scalar_prefetch=5,
        grid=(count,),
        in_specs=[
            pl.BlockSpec((1, width, width), lambda i, od, ls, rs, ow, lv: (od[i], 0, 0)),
            pl.BlockSpec((1, chans, width, width), lambda i, od, ls, rs, ow, lv: (ow[ls[od[i]]], 0, 0, 0)),
            pl.BlockSpec((1, chans, width, width), lambda i, od, ls, rs, ow, lv: (ow[rs[od[i]]], 1, 0, 0)),
        ],
        out_specs=pl.BlockSpec((1, width, width), lambda i, od, ls, rs, ow, lv: (od[i], 0, 0)),
    )
    flops = count * chans * 4 * width ** 3
    nbytes = count * (2 * chans + 2) * width * width * 2
    return pl.pallas_call(
        block_kernel,
        grid_spec=grid_spec,
        out_shape=jax.ShapeDtypeStruct((count, width, width), jnp.bfloat16),
        cost_estimate=pl.CostEstimate(flops=flops, bytes_accessed=nbytes, transcendentals=0),
    )(order, lsec, rsec, owner, live, psi, both, both)


def by_left_sector(lsec):
    count = lsec.shape[0]
    pos = jnp.arange(count, dtype=jnp.int32)
    before = (lsec[None, :] < lsec[:, None]) | ((lsec[None, :] == lsec[:, None]) & (pos[None, :] < pos[:, None]))
    rank = jnp.sum(before.astype(jnp.int32), axis=1)
    return jnp.sum(jnp.where(rank[None, :] == pos[:, None], pos[None, :], 0), axis=1)


def on_device(psi, left_env, right_env, left_sector, right_sector, sector_owner, sector_rows):
    nenv = lax.axis_size("env")
    count, width, _ = psi.shape
    lsec = left_sector[:, 0]
    rsec = right_sector[:, 0]
    order = by_left_sector(lsec)
    both = gather_env(jnp.concatenate([left_env[:, 0], right_env[:, 0]], axis=0))
    part = apply_blocks(psi, both, order, lsec, rsec, sector_owner, sector_rows)
    share = width // nenv
    part = part.reshape(count, nenv, share, width)
    got = lax.all_to_all(part, "env", split_axis=1, concat_axis=1, tiled=True)
    total = jnp.sum(got.astype(jnp.float32), axis=1)
    return total.astype(jnp.bfloat16)


def solution(mesh):
    nenv, nwave = mesh.devices.shape
    split = jax.sharding.Mesh(mesh.devices.reshape(nenv, NY, NZ, 2), ("env", "y", "z", "core"))
    wave = ("y", "z", "core")
    return jax.shard_map(
        on_device,
        mesh=split,
        in_specs=(
            P(wave, None, None),
            P("env", wave, None, None),
            P("env", wave, None, None),
            P(wave, None),
            P(wave, None),
            P(),
            P(),
        ),
        out_specs=P(wave, "env", None),
        check_vma=False,
    )
```

```python
import functools

import jax
import jax.numpy as jnp
from jax import lax
from jax.experimental import pallas as pl
from jax.experimental.pallas import tpu as pltpu
from jax.sharding import PartitionSpec as P

MESH = pl.DeviceIdType.MESH
NY, NZ = 4, 8


def gather_kernel(x_ref, g_ref, own_sem, recv, sent):
    e = lax.axis_index("env")
    y = lax.axis_index("y")
    z = lax.axis_index("z")
    c = lax.axis_index("core")
    half = x_ref.shape[0] // 2

    def dev(yy, zz, cc):
        return (e, lax.rem(yy + 2 * NY, NY), lax.rem(zz + 2 * NZ, NZ), cc)

    def slot(yy, zz, cc):
        return (lax.rem(yy + 2 * NY, NY) * NZ + lax.rem(zz + 2 * NZ, NZ)) * 2 + cc

    barrier = pltpu.get_barrier_semaphore()
    peers = [dev(y + 1, z, c), dev(y - 1, z, c), dev(y, z + 1, c), dev(y, z - 1, c), dev(y, z, 1 - c)]
    for p in peers:
        pl.semaphore_signal(barrier, inc=1, device_id=p, device_id_type=MESH)
    pl.semaphore_wait(barrier, len(peers))

    own = pltpu.make_async_copy(x_ref, g_ref.at[slot(y, z, c)], own_sem)
    own.start()

    def role(cc, first, second):
        fsize, fstep = first
        ssize, sstep = second
        fplus, fminus = fsize // 2, fsize - 1 - fsize // 2
        splus, sminus = ssize // 2, ssize - 1 - ssize // 2
        sends = []
        partner = dev(y, z, 1 - cc)

        def where(a, b, h):
            sign = 1 - 2 * h
            fy, fz = fstep(sign * a)
            sy, sz = sstep(sign * b)
            return y - fy - sy, z - fz - sz

        def part(ref, h):
            return ref.at[pl.ds(h * half, half)]

        def item(a, b, h):
            oy, oz = where(a, b, h)
            return slot(oy, oz, cc)

        def near(h, ring, d):
            sign = 1 - 2 * h
            dy, dz = ring(sign * d)
            return dev(y + dy, z + dz, cc)

        def send(src, a, b, h, target, kind):
            s = item(a, b, h)
            cp = pltpu.make_async_remote_copy(
                src_ref=src, dst_ref=part(g_ref.at[s], h), send_sem=sent.at[s, h, kind],
                recv_sem=recv.at[s, h], device_id=target, device_id_type=MESH)
            cp.start()
            sends.append(cp)

        def wait_in(s, h):
            cp = pltpu.make_async_remote_copy(
                src_ref=part(g_ref.at[s], h), dst_ref=part(g_ref.at[s], h), send_sem=sent.at[s, h, 0],
                recv_sem=recv.at[s, h], device_id=partner, device_id_type=MESH)
            cp.wait_recv()

        def held(a, b, h):
            return part(g_ref.at[item(a, b, h)], h)

        def spread(src, a, b, h):
            if b == 0:
                send(src, a, 0, h, near(h, sstep, 1), 2)
                send(src, a, 0, h, near(h, sstep, -1), 3)
            elif 0 < b < splus:
                send(src, a, b, h, near(h, sstep, 1), 2)
            elif 0 < -b < sminus:
                send(src, a, b, h, near(h, sstep, -1), 3)
            send(src, a, b, h, partner, 4)

        for h in range(2):
            send(part(x_ref, h), 0, 0, h, near(h, fstep, 1), 0)
            send(part(x_ref, h), 0, 0, h, near(h, fstep, -1), 1)
        for h in range(2):
            spread(part(x_ref, h), 0, 0, h)
        for step in range(1, max(fplus, fminus) + 1):
            for a in (step, -step):
                if (a > 0 and a > fplus) or (a < 0 and -a > fminus):
                    continue
                for h in range(2):
                    wait_in(item(a, 0, h), h)
                    if 0 < a < fplus:
                        send(held(a, 0, h), a, 0, h, near(h, fstep, 1), 0)
                    if 0 < -a < fminus:
                        send(held(a, 0, h), a, 0, h, near(h, fstep, -1), 1)
                    spread(held(a, 0, h), a, 0, h)
        row = list(range(-fminus, fplus + 1))
        for step in range(1, max(splus, sminus) + 1):
            for b in (step, -step):
                if (b > 0 and b > splus) or (b < 0 and -b > sminus):
                    continue
                for a in row:
                    for h in range(2):
                        wait_in(item(a, b, h), h)
                        spread(held(a, b, h), a, b, h)
        for yy in range(NY):
            for zz in range(NZ):
                for h in range(2):
                    wait_in((yy * NZ + zz) * 2 + (1 - cc), h)
        for cp in sends:
            cp.wait_send()

    zstep = lambda d: (0, d)
    ystep = lambda d: (d, 0)

    @pl.when(c == 0)
    def _():
        role(0, (NZ, zstep), (NY, ystep))

    @pl.when(c == 1)
    def _():
        role(1, (NY, ystep), (NZ, zstep))

    own.wait()


def gather_env(x):
    shape = (NY * NZ * 2,) + x.shape
    return pl.pallas_call(
        gather_kernel,
        out_shape=jax.ShapeDtypeStruct(shape, x.dtype),
        in_specs=[pl.BlockSpec(memory_space=pl.ANY)],
        out_specs=pl.BlockSpec(memory_space=pl.ANY),
        scratch_shapes=[
            pltpu.SemaphoreType.DMA(()),
            pltpu.SemaphoreType.DMA((NY * NZ * 2, 2)),
            pltpu.SemaphoreType.DMA((NY * NZ * 2, 2, 5)),
        ],
        compiler_params=pltpu.CompilerParams(collective_id=0, has_side_effects=True),
    )(x)


def block_kernel(lsec, rsec, owner, live, psi_ref, *refs):
    group = psi_ref.shape[0]
    width = psi_ref.shape[1]
    env_refs, out_ref = refs[:-1], refs[-1]
    rows = lax.broadcasted_iota(jnp.int32, (width, width), 0)
    cols = lax.broadcasted_iota(jnp.int32, (width, width), 1)
    for j in range(group):
        k = pl.program_id(0) * group + j
        l_ref, r_ref = env_refs[2 * j], env_refs[2 * j + 1]
        mask = (rows < live[lsec[k]]) & (cols < live[rsec[k]])
        masked = jnp.where(mask, psi_ref[j], jnp.zeros_like(psi_ref[j]))
        chans = l_ref.shape[1]
        lmat = l_ref[...].reshape(chans * width, width)
        y = jnp.dot(lmat, masked, preferred_element_type=jnp.float32).astype(jnp.bfloat16)
        ywide = jnp.concatenate([y[w * width:(w + 1) * width] for w in range(chans)], axis=1)
        rmat = r_ref[...].reshape(chans * width, width)
        acc = jnp.dot(ywide, rmat, preferred_element_type=jnp.float32)
        out_ref[j] = jnp.where(mask, acc, 0.0).astype(out_ref.dtype)


def apply_blocks(psi, both, lsec, rsec, owner, live, group=4):
    count, width, _ = psi.shape
    chans = both.shape[1] // 2
    env_specs = []
    for j in range(group):
        env_specs.append(pl.BlockSpec(
            (1, chans, width, width), lambda i, ls, rs, ow, lv, j=j: (ow[ls[i * group + j]], 0, 0, 0)))
        env_specs.append(pl.BlockSpec(
            (1, chans, width, width), lambda i, ls, rs, ow, lv, j=j: (ow[rs[i * group + j]], 1, 0, 0)))
    grid_spec = pltpu.PrefetchScalarGridSpec(
        num_scalar_prefetch=4,
        grid=(count // group,),
        in_specs=[pl.BlockSpec((group, width, width), lambda i, ls, rs, ow, lv: (i, 0, 0))] + env_specs,
        out_specs=pl.BlockSpec((group, width, width), lambda i, ls, rs, ow, lv: (i, 0, 0)),
    )
    flops = count * chans * 4 * width ** 3
    nbytes = count * (2 * chans + 2) * width * width * 2
    return pl.pallas_call(
        block_kernel,
        grid_spec=grid_spec,
        out_shape=jax.ShapeDtypeStruct((count, width, width), jnp.bfloat16),
        cost_estimate=pl.CostEstimate(flops=flops, bytes_accessed=nbytes, transcendentals=0),
    )(lsec, rsec, owner, live, psi, *([both] * (2 * group)))


def on_device(psi, left_env, right_env, left_sector, right_sector, sector_owner, sector_rows):
    nenv = lax.axis_size("env")
    count, width, _ = psi.shape
    lsec = left_sector[:, 0]
    rsec = right_sector[:, 0]
    both = gather_env(jnp.concatenate([left_env[:, 0], right_env[:, 0]], axis=0))
    part = apply_blocks(psi, both, lsec, rsec, sector_owner, sector_rows)
    share = width // nenv
    part = part.reshape(count, nenv, share, width)
    got = lax.all_to_all(part, "env", split_axis=1, concat_axis=1, tiled=True)
    total = jnp.sum(got.astype(jnp.float32), axis=1)
    return total.astype(jnp.bfloat16)


def solution(mesh):
    nenv, nwave = mesh.devices.shape
    split = jax.sharding.Mesh(mesh.devices.reshape(nenv, NY, NZ, 2), ("env", "y", "z", "core"))
    wave = ("y", "z", "core")
    return jax.shard_map(
        on_device,
        mesh=split,
        in_specs=(
            P(wave, None, None),
            P("env", wave, None, None),
            P("env", wave, None, None),
            P(wave, None),
            P(wave, None),
            P(),
            P(),
        ),
        out_specs=P(wave, "env", None),
        check_vma=False,
    )
```

```python
import functools

import jax
import jax.numpy as jnp
from jax import lax
from jax.experimental import pallas as pl
from jax.experimental.pallas import tpu as pltpu
from jax.sharding import PartitionSpec as P

MESH = pl.DeviceIdType.MESH
NY, NZ = 4, 8


def gather_kernel(l_ref, r_ref, g_ref, own_sem, recv, sent):
    e = lax.axis_index("env")
    y = lax.axis_index("y")
    z = lax.axis_index("z")
    c = lax.axis_index("core")
    half = l_ref.shape[0]
    shards = (l_ref, r_ref)

    def dev(yy, zz, cc):
        return (e, lax.rem(yy + 2 * NY, NY), lax.rem(zz + 2 * NZ, NZ), cc)

    def slot(yy, zz, cc):
        return (lax.rem(yy + 2 * NY, NY) * NZ + lax.rem(zz + 2 * NZ, NZ)) * 2 + cc

    barrier = pltpu.get_barrier_semaphore()
    peers = [dev(y + 1, z, c), dev(y - 1, z, c), dev(y, z + 1, c), dev(y, z - 1, c), dev(y, z, 1 - c)]
    for p in peers:
        pl.semaphore_signal(barrier, inc=1, device_id=p, device_id_type=MESH)
    pl.semaphore_wait(barrier, len(peers))

    owns = []
    for h in range(2):
        cp = pltpu.make_async_copy(shards[h], g_ref.at[slot(y, z, c), pl.ds(h * half, half)], own_sem.at[h])
        cp.start()
        owns.append(cp)

    def role(cc, first, second):
        fsize, fstep = first
        ssize, sstep = second
        fplus, fminus = fsize // 2, fsize - 1 - fsize // 2
        splus, sminus = ssize // 2, ssize - 1 - ssize // 2
        sends = []
        partner = dev(y, z, 1 - cc)

        def where(a, b, h):
            sign = 1 - 2 * h
            fy, fz = fstep(sign * a)
            sy, sz = sstep(sign * b)
            return y - fy - sy, z - fz - sz

        def part(ref, h):
            return ref.at[pl.ds(h * half, half)]

        def item(a, b, h):
            oy, oz = where(a, b, h)
            return slot(oy, oz, cc)

        def near(h, ring, d):
            sign = 1 - 2 * h
            dy, dz = ring(sign * d)
            return dev(y + dy, z + dz, cc)

        def send(src, a, b, h, target, kind):
            s = item(a, b, h)
            cp = pltpu.make_async_remote_copy(
                src_ref=src, dst_ref=part(g_ref.at[s], h), send_sem=sent.at[s, h, kind],
                recv_sem=recv.at[s, h], device_id=target, device_id_type=MESH)
            cp.start()
            sends.append(cp)

        def wait_in(s, h):
            cp = pltpu.make_async_remote_copy(
                src_ref=part(g_ref.at[s], h), dst_ref=part(g_ref.at[s], h), send_sem=sent.at[s, h, 0],
                recv_sem=recv.at[s, h], device_id=partner, device_id_type=MESH)
            cp.wait_recv()

        def held(a, b, h):
            return part(g_ref.at[item(a, b, h)], h)

        def spread(src, a, b, h):
            if b == 0:
                send(src, a, 0, h, near(h, sstep, 1), 2)
                send(src, a, 0, h, near(h, sstep, -1), 3)
            elif 0 < b < splus:
                send(src, a, b, h, near(h, sstep, 1), 2)
            elif 0 < -b < sminus:
                send(src, a, b, h, near(h, sstep, -1), 3)
            send(src, a, b, h, partner, 4)

        for h in range(2):
            send(shards[h], 0, 0, h, near(h, fstep, 1), 0)
            send(shards[h], 0, 0, h, near(h, fstep, -1), 1)
        for h in range(2):
            spread(shards[h], 0, 0, h)
        for step in range(1, max(fplus, fminus) + 1):
            for a in (step, -step):
                if (a > 0 and a > fplus) or (a < 0 and -a > fminus):
                    continue
                for h in range(2):
                    wait_in(item(a, 0, h), h)
                    if 0 < a < fplus:
                        send(held(a, 0, h), a, 0, h, near(h, fstep, 1), 0)
                    if 0 < -a < fminus:
                        send(held(a, 0, h), a, 0, h, near(h, fstep, -1), 1)
                    spread(held(a, 0, h), a, 0, h)
        row = list(range(-fminus, fplus + 1))
        for step in range(1, max(splus, sminus) + 1):
            for b in (step, -step):
                if (b > 0 and b > splus) or (b < 0 and -b > sminus):
                    continue
                for a in row:
                    for h in range(2):
                        wait_in(item(a, b, h), h)
                        spread(held(a, b, h), a, b, h)
        for yy in range(NY):
            for zz in range(NZ):
                for h in range(2):
                    wait_in((yy * NZ + zz) * 2 + (1 - cc), h)
        for cp in sends:
            cp.wait_send()

    zstep = lambda d: (0, d)
    ystep = lambda d: (d, 0)

    @pl.when(c == 0)
    def _():
        role(0, (NZ, zstep), (NY, ystep))

    @pl.when(c == 1)
    def _():
        role(1, (NY, ystep), (NZ, zstep))

    for cp in owns:
        cp.wait()


def gather_env(left, right):
    shape = (NY * NZ * 2, 2 * left.shape[0]) + left.shape[1:]
    return pl.pallas_call(
        gather_kernel,
        out_shape=jax.ShapeDtypeStruct(shape, left.dtype),
        in_specs=[pl.BlockSpec(memory_space=pl.ANY)] * 2,
        out_specs=pl.BlockSpec(memory_space=pl.ANY),
        scratch_shapes=[
            pltpu.SemaphoreType.DMA((2,)),
            pltpu.SemaphoreType.DMA((NY * NZ * 2, 2)),
            pltpu.SemaphoreType.DMA((NY * NZ * 2, 2, 5)),
        ],
        compiler_params=pltpu.CompilerParams(collective_id=0, has_side_effects=True),
    )(left, right)


def block_kernel(lsec, rsec, owner, live, psi_ref, *refs):
    group = psi_ref.shape[0]
    width = psi_ref.shape[1]
    env_refs, out_ref = refs[:-1], refs[-1]
    rows = lax.broadcasted_iota(jnp.int32, (width, width), 0)
    cols = lax.broadcasted_iota(jnp.int32, (width, width), 1)
    for j in range(group):
        k = pl.program_id(0) * group + j
        l_ref, r_ref = env_refs[2 * j], env_refs[2 * j + 1]
        mask = (rows < live[lsec[k]]) & (cols < live[rsec[k]])
        masked = jnp.where(mask, psi_ref[j], jnp.zeros_like(psi_ref[j]))
        chans = l_ref.shape[1]
        lmat = l_ref[...].reshape(chans * width, width)
        y = jnp.dot(lmat, masked, preferred_element_type=jnp.float32).astype(jnp.bfloat16)
        ywide = jnp.concatenate([y[w * width:(w + 1) * width] for w in range(chans)], axis=1)
        rmat = r_ref[...].reshape(chans * width, width)
        acc = jnp.dot(ywide, rmat, preferred_element_type=jnp.float32)
        out_ref[j] = jnp.where(mask, acc, 0.0).astype(out_ref.dtype)


def apply_blocks(psi, both, lsec, rsec, owner, live, group=8):
    count, width, _ = psi.shape
    chans = both.shape[1] // 2
    env_specs = []
    for j in range(group):
        env_specs.append(pl.BlockSpec(
            (1, chans, width, width), lambda i, ls, rs, ow, lv, j=j: (ow[ls[i * group + j]], 0, 0, 0)))
        env_specs.append(pl.BlockSpec(
            (1, chans, width, width), lambda i, ls, rs, ow, lv, j=j: (ow[rs[i * group + j]], 1, 0, 0)))
    grid_spec = pltpu.PrefetchScalarGridSpec(
        num_scalar_prefetch=4,
        grid=(count // group,),
        in_specs=[pl.BlockSpec((group, width, width), lambda i, ls, rs, ow, lv: (i, 0, 0))] + env_specs,
        out_specs=pl.BlockSpec((group, width, width), lambda i, ls, rs, ow, lv: (i, 0, 0)),
    )
    flops = count * chans * 4 * width ** 3
    nbytes = count * (2 * chans + 2) * width * width * 2
    return pl.pallas_call(
        block_kernel,
        grid_spec=grid_spec,
        out_shape=jax.ShapeDtypeStruct((count, width, width), jnp.bfloat16),
        cost_estimate=pl.CostEstimate(flops=flops, bytes_accessed=nbytes, transcendentals=0),
    )(lsec, rsec, owner, live, psi, *([both] * (2 * group)))


def on_device(psi, left_env, right_env, left_sector, right_sector, sector_owner, sector_rows):
    nenv = lax.axis_size("env")
    count, width, _ = psi.shape
    lsec = left_sector[:, 0]
    rsec = right_sector[:, 0]
    both = gather_env(left_env[:, 0], right_env[:, 0])
    part = apply_blocks(psi, both, lsec, rsec, sector_owner, sector_rows)
    share = width // nenv
    part = part.reshape(count, nenv, share, width)
    got = lax.all_to_all(part, "env", split_axis=1, concat_axis=1, tiled=True)
    total = jnp.sum(got.astype(jnp.float32), axis=1)
    return total.astype(jnp.bfloat16)


def solution(mesh):
    nenv, nwave = mesh.devices.shape
    split = jax.sharding.Mesh(mesh.devices.reshape(nenv, NY, NZ, 2), ("env", "y", "z", "core"))
    wave = ("y", "z", "core")
    return jax.shard_map(
        on_device,
        mesh=split,
        in_specs=(
            P(wave, None, None),
            P("env", wave, None, None),
            P("env", wave, None, None),
            P(wave, None),
            P(wave, None),
            P(),
            P(),
        ),
        out_specs=P(wave, "env", None),
        check_vma=False,
    )
```

```python
import functools

import jax
import jax.numpy as jnp
from jax import lax
from jax.experimental import pallas as pl
from jax.experimental.pallas import tpu as pltpu
from jax.sharding import PartitionSpec as P

MESH = pl.DeviceIdType.MESH
NY, NZ = 4, 8


def gather_kernel(l_ref, r_ref, g_ref, own_sem, recv, sent):
    e = lax.axis_index("env")
    y = lax.axis_index("y")
    z = lax.axis_index("z")
    c = lax.axis_index("core")
    half = l_ref.shape[0]
    shards = (l_ref, r_ref)

    def dev(yy, zz, cc):
        return (e, lax.rem(yy + 2 * NY, NY), lax.rem(zz + 2 * NZ, NZ), cc)

    def slot(yy, zz, cc):
        return (lax.rem(yy + 2 * NY, NY) * NZ + lax.rem(zz + 2 * NZ, NZ)) * 2 + cc

    barrier = pltpu.get_barrier_semaphore()
    peers = [dev(y + 1, z, c), dev(y - 1, z, c), dev(y, z + 1, c), dev(y, z - 1, c), dev(y, z, 1 - c)]
    for p in peers:
        pl.semaphore_signal(barrier, inc=1, device_id=p, device_id_type=MESH)
    pl.semaphore_wait(barrier, len(peers))

    owns = []
    for h in range(2):
        cp = pltpu.make_async_copy(shards[h], g_ref.at[slot(y, z, c), pl.ds(h * half, half)], own_sem.at[h])
        cp.start()
        owns.append(cp)

    def role(cc, first, second):
        fsize, fstep = first
        ssize, sstep = second
        fplus, fminus = fsize // 2, fsize - 1 - fsize // 2
        splus, sminus = ssize // 2, ssize - 1 - ssize // 2
        sends = []
        partner = dev(y, z, 1 - cc)

        def where(a, b, h):
            sign = 1 - 2 * h
            fy, fz = fstep(sign * a)
            sy, sz = sstep(sign * b)
            return y - fy - sy, z - fz - sz

        def part(ref, h):
            return ref.at[pl.ds(h * half, half)]

        def item(a, b, h):
            oy, oz = where(a, b, h)
            return slot(oy, oz, cc)

        def near(h, ring, d):
            sign = 1 - 2 * h
            dy, dz = ring(sign * d)
            return dev(y + dy, z + dz, cc)

        def send(src, a, b, h, target, kind):
            s = item(a, b, h)
            cp = pltpu.make_async_remote_copy(
                src_ref=src, dst_ref=part(g_ref.at[s], h), send_sem=sent.at[s, h, kind],
                recv_sem=recv.at[s, h], device_id=target, device_id_type=MESH)
            cp.start()
            sends.append(cp)

        def wait_in(s, h):
            cp = pltpu.make_async_remote_copy(
                src_ref=part(g_ref.at[s], h), dst_ref=part(g_ref.at[s], h), send_sem=sent.at[s, h, 0],
                recv_sem=recv.at[s, h], device_id=partner, device_id_type=MESH)
            cp.wait_recv()

        def held(a, b, h):
            return part(g_ref.at[item(a, b, h)], h)

        def spread(src, a, b, h):
            if b == 0:
                send(src, a, 0, h, near(h, sstep, 1), 2)
                send(src, a, 0, h, near(h, sstep, -1), 3)
            elif 0 < b < splus:
                send(src, a, b, h, near(h, sstep, 1), 2)
            elif 0 < -b < sminus:
                send(src, a, b, h, near(h, sstep, -1), 3)
            send(src, a, b, h, partner, 4)

        for h in range(2):
            send(shards[h], 0, 0, h, near(h, fstep, 1), 0)
            send(shards[h], 0, 0, h, near(h, fstep, -1), 1)
        for h in range(2):
            spread(shards[h], 0, 0, h)
        for step in range(1, max(fplus, fminus) + 1):
            for a in (step, -step):
                if (a > 0 and a > fplus) or (a < 0 and -a > fminus):
                    continue
                for h in range(2):
                    wait_in(item(a, 0, h), h)
                    if 0 < a < fplus:
                        send(held(a, 0, h), a, 0, h, near(h, fstep, 1), 0)
                    if 0 < -a < fminus:
                        send(held(a, 0, h), a, 0, h, near(h, fstep, -1), 1)
                    spread(held(a, 0, h), a, 0, h)
        row = list(range(-fminus, fplus + 1))
        for step in range(1, max(splus, sminus) + 1):
            for b in (step, -step):
                if (b > 0 and b > splus) or (b < 0 and -b > sminus):
                    continue
                for a in row:
                    for h in range(2):
                        wait_in(item(a, b, h), h)
                        spread(held(a, b, h), a, b, h)
        for yy in range(NY):
            for zz in range(NZ):
                for h in range(2):
                    wait_in((yy * NZ + zz) * 2 + (1 - cc), h)
        for cp in sends:
            cp.wait_send()

    zstep = lambda d: (0, d)
    ystep = lambda d: (d, 0)

    @pl.when(c == 0)
    def _():
        role(0, (NZ, zstep), (NY, ystep))

    @pl.when(c == 1)
    def _():
        role(1, (NY, ystep), (NZ, zstep))

    for cp in owns:
        cp.wait()


def gather_env(left, right):
    shape = (NY * NZ * 2, 2 * left.shape[0]) + left.shape[1:]
    return pl.pallas_call(
        gather_kernel,
        out_shape=jax.ShapeDtypeStruct(shape, left.dtype),
        in_specs=[pl.BlockSpec(memory_space=pl.ANY)] * 2,
        out_specs=pl.BlockSpec(memory_space=pl.ANY),
        scratch_shapes=[
            pltpu.SemaphoreType.DMA((2,)),
            pltpu.SemaphoreType.DMA((NY * NZ * 2, 2)),
            pltpu.SemaphoreType.DMA((NY * NZ * 2, 2, 5)),
        ],
        compiler_params=pltpu.CompilerParams(collective_id=0, has_side_effects=True),
    )(left, right)


def block_kernel(lsec, rsec, owner, live, psi_ref, *refs):
    group = psi_ref.shape[0]
    width = psi_ref.shape[1]
    env_refs, out_ref = refs[:-1], refs[-1]
    rows = lax.broadcasted_iota(jnp.int32, (width, width), 0)
    cols = lax.broadcasted_iota(jnp.int32, (width, width), 1)
    for j in range(group):
        k = pl.program_id(0) * group + j
        l_ref, r_ref = env_refs[2 * j], env_refs[2 * j + 1]
        mask = (rows < live[lsec[k]]) & (cols < live[rsec[k]])
        masked = jnp.where(mask, psi_ref[j], jnp.zeros_like(psi_ref[j]))
        chans = l_ref.shape[1]
        lmat = l_ref[...].reshape(chans * width, width)
        y = jnp.dot(lmat, masked, preferred_element_type=jnp.float32).astype(jnp.bfloat16)
        ywide = jnp.concatenate([y[w * width:(w + 1) * width] for w in range(chans)], axis=1)
        rmat = r_ref[...].reshape(chans * width, width)
        acc = jnp.dot(ywide, rmat, preferred_element_type=jnp.float32)
        part = jnp.where(mask, acc, 0.0).astype(out_ref.dtype)
        share = out_ref.shape[2]
        for r in range(out_ref.shape[0]):
            out_ref[r, j] = part[r * share:(r + 1) * share]


def apply_blocks(psi, both, lsec, rsec, owner, live, nenv, group=8):
    count, width, _ = psi.shape
    share = width // nenv
    chans = both.shape[1] // 2
    env_specs = []
    for j in range(group):
        env_specs.append(pl.BlockSpec(
            (1, chans, width, width), lambda i, ls, rs, ow, lv, j=j: (ow[ls[i * group + j]], 0, 0, 0)))
        env_specs.append(pl.BlockSpec(
            (1, chans, width, width), lambda i, ls, rs, ow, lv, j=j: (ow[rs[i * group + j]], 1, 0, 0)))
    grid_spec = pltpu.PrefetchScalarGridSpec(
        num_scalar_prefetch=4,
        grid=(count // group,),
        in_specs=[pl.BlockSpec((group, width, width), lambda i, ls, rs, ow, lv: (i, 0, 0))] + env_specs,
        out_specs=pl.BlockSpec((nenv, group, share, width), lambda i, ls, rs, ow, lv: (0, i, 0, 0)),
    )
    flops = count * chans * 4 * width ** 3
    nbytes = count * (2 * chans + 2) * width * width * 2
    return pl.pallas_call(
        block_kernel,
        grid_spec=grid_spec,
        out_shape=jax.ShapeDtypeStruct((nenv, count, share, width), jnp.bfloat16),
        cost_estimate=pl.CostEstimate(flops=flops, bytes_accessed=nbytes, transcendentals=0),
    )(lsec, rsec, owner, live, psi, *([both] * (2 * group)))


def exchange_kernel(part_ref, out_ref, got, relay, own_sem, recv_sem, relay_sem, sent):
    nenv, count, share, width = part_ref.shape
    e = lax.axis_index("env")
    y = lax.axis_index("y")
    z = lax.axis_index("z")
    c = lax.axis_index("core")
    half = count // 2

    def at(d):
        return lax.rem(e + d + 2 * nenv, nenv)

    def dev(d):
        return (at(d), y, z, c)

    barrier = pltpu.get_barrier_semaphore()
    for d in (1, -1):
        pl.semaphore_signal(barrier, inc=1, device_id=dev(d), device_id_type=MESH)
    pl.semaphore_wait(barrier, 2)

    own = pltpu.make_async_copy(part_ref.at[e], got.at[e], own_sem)
    own.start()

    def remote(src, dst, rsem, ssem, d):
        return pltpu.make_async_remote_copy(
            src_ref=src, dst_ref=dst, send_sem=ssem, recv_sem=rsem,
            device_id=dev(d), device_id_type=MESH)

    lo, hi = pl.ds(0, half), pl.ds(half, half)
    sends = [
        remote(part_ref.at[at(1)], got.at[e], recv_sem.at[0], sent.at[0], 1),
        remote(part_ref.at[at(-1)], got.at[e], recv_sem.at[1], sent.at[1], -1),
        remote(part_ref.at[at(2), lo], relay.at[0], relay_sem.at[0], sent.at[2], 1),
        remote(part_ref.at[at(2), hi], relay.at[1], relay_sem.at[1], sent.at[3], -1),
    ]
    for cp in sends:
        cp.start()
    remote(relay.at[0], relay.at[0], relay_sem.at[0], sent.at[2], 1).wait_recv()
    fwd_up = remote(relay.at[0], got.at[at(-1), lo], recv_sem.at[2], sent.at[4], 1)
    fwd_up.start()
    remote(relay.at[1], relay.at[1], relay_sem.at[1], sent.at[3], -1).wait_recv()
    fwd_down = remote(relay.at[1], got.at[at(1), hi], recv_sem.at[3], sent.at[5], -1)
    fwd_down.start()
    remote(got.at[at(-1)], got.at[at(-1)], recv_sem.at[0], sent.at[0], -1).wait_recv()
    remote(got.at[at(1)], got.at[at(1)], recv_sem.at[1], sent.at[1], 1).wait_recv()
    remote(got.at[at(2), lo], got.at[at(2), lo], recv_sem.at[2], sent.at[4], -1).wait_recv()
    remote(got.at[at(2), hi], got.at[at(2), hi], recv_sem.at[3], sent.at[5], 1).wait_recv()
    own.wait()
    for cp in sends + [fwd_up, fwd_down]:
        cp.wait_send()

    def body(j, carry):
        total = got[0, j].astype(jnp.float32)
        for s in range(1, nenv):
            total = total + got[s, j].astype(jnp.float32)
        out_ref[j] = total.astype(out_ref.dtype)
        return carry

    lax.fori_loop(0, count, body, 0)


def exchange(part):
    nenv, count, share, width = part.shape
    return pl.pallas_call(
        exchange_kernel,
        out_shape=jax.ShapeDtypeStruct((count, share, width), part.dtype),
        in_specs=[pl.BlockSpec(memory_space=pl.ANY)],
        out_specs=pl.BlockSpec(memory_space=pltpu.VMEM),
        scratch_shapes=[
            pltpu.VMEM((nenv, count, share, width), part.dtype),
            pltpu.VMEM((2, count // 2, share, width), part.dtype),
            pltpu.SemaphoreType.DMA(()),
            pltpu.SemaphoreType.DMA((4,)),
            pltpu.SemaphoreType.DMA((2,)),
            pltpu.SemaphoreType.DMA((6,)),
        ],
        compiler_params=pltpu.CompilerParams(collective_id=1, has_side_effects=True),
    )(part)


def on_device(psi, left_env, right_env, left_sector, right_sector, sector_owner, sector_rows):
    nenv = lax.axis_size("env")
    count, width, _ = psi.shape
    lsec = left_sector[:, 0]
    rsec = right_sector[:, 0]
    both = gather_env(left_env[:, 0], right_env[:, 0])
    part = apply_blocks(psi, both, lsec, rsec, sector_owner, sector_rows, nenv)
    return exchange(part)


def solution(mesh):
    nenv, nwave = mesh.devices.shape
    split = jax.sharding.Mesh(mesh.devices.reshape(nenv, NY, NZ, 2), ("env", "y", "z", "core"))
    wave = ("y", "z", "core")
    return jax.shard_map(
        on_device,
        mesh=split,
        in_specs=(
            P(wave, None, None),
            P("env", wave, None, None),
            P("env", wave, None, None),
            P(wave, None),
            P(wave, None),
            P(),
            P(),
        ),
        out_specs=P(wave, "env", None),
        check_vma=False,
    )
```

```python
import functools

import jax
import jax.numpy as jnp
from jax import lax
from jax.experimental import pallas as pl
from jax.experimental.pallas import tpu as pltpu
from jax.sharding import PartitionSpec as P

MESH = pl.DeviceIdType.MESH
NY, NZ = 4, 8


PIECES = (
    ((0, 10, 1, "zy"), (10, 10, -1, "zy")),
    ((0, 8, 1, "yz"), (8, 2, 1, "zy"), (10, 8, -1, "yz"), (18, 2, -1, "zy")),
)


def gather_kernel(l_ref, r_ref, g_ref, own_sem, recv, sent):
    e = lax.axis_index("env")
    y = lax.axis_index("y")
    z = lax.axis_index("z")
    c = lax.axis_index("core")
    half = l_ref.shape[0]

    def dev(yy, zz, cc):
        return (e, lax.rem(yy + 2 * NY, NY), lax.rem(zz + 2 * NZ, NZ), cc)

    def slot(yy, zz, cc):
        return (lax.rem(yy + 2 * NY, NY) * NZ + lax.rem(zz + 2 * NZ, NZ)) * 2 + cc

    barrier = pltpu.get_barrier_semaphore()
    peers = [dev(y + 1, z, c), dev(y - 1, z, c), dev(y, z + 1, c), dev(y, z - 1, c), dev(y, z, 1 - c)]
    for p in peers:
        pl.semaphore_signal(barrier, inc=1, device_id=p, device_id_type=MESH)
    pl.semaphore_wait(barrier, len(peers))

    owns = []
    for h, src in enumerate((l_ref, r_ref)):
        cp = pltpu.make_async_copy(src, g_ref.at[slot(y, z, c), pl.ds(h * half, half)], own_sem.at[h])
        cp.start()
        owns.append(cp)

    def own_part(lo, n):
        if lo < half:
            return l_ref.at[pl.ds(lo, n)]
        return r_ref.at[pl.ds(lo - half, n)]

    zstep = lambda d: (0, d)
    ystep = lambda d: (d, 0)
    rings = {"z": (NZ, zstep), "y": (NY, ystep)}

    def role(cc):
        sends = []
        partner = dev(y, z, 1 - cc)
        levels = {}

        for pi, (lo, n, sign, order) in enumerate(PIECES[cc]):
            fsize, fstep = rings[order[0]]
            ssize, sstep = rings[order[1]]
            fplus, fminus = fsize // 2, fsize - 1 - fsize // 2
            splus, sminus = ssize // 2, ssize - 1 - ssize // 2

            def item(a, b, fstep=fstep, sstep=sstep, sign=sign):
                fy, fz = fstep(sign * a)
                sy, sz = sstep(sign * b)
                return slot(y - fy - sy, z - fz - sz, cc)

            def near(ring, d, sign=sign):
                dy, dz = ring(sign * d)
                return dev(y + dy, z + dz, cc)

            def send(src, a, b, target, kind, pi=pi, lo=lo, n=n, item=item):
                s = item(a, b)
                cp = pltpu.make_async_remote_copy(
                    src_ref=src, dst_ref=g_ref.at[s, pl.ds(lo, n)], send_sem=sent.at[s, pi, kind],
                    recv_sem=recv.at[s, pi], device_id=target, device_id_type=MESH)
                cp.start()
                sends.append(cp)

            def handle(a, b, wait, pi=pi, lo=lo, n=n, item=item, near=near, send=send,
                       fstep=fstep, sstep=sstep, fplus=fplus, fminus=fminus, splus=splus, sminus=sminus):
                if wait:
                    s = item(a, b)
                    pltpu.make_async_remote_copy(
                        src_ref=g_ref.at[s, pl.ds(lo, n)], dst_ref=g_ref.at[s, pl.ds(lo, n)],
                        send_sem=sent.at[s, pi, 0], recv_sem=recv.at[s, pi], device_id=partner,
                        device_id_type=MESH).wait_recv()
                    src = g_ref.at[s, pl.ds(lo, n)]
                else:
                    src = own_part(lo, n)
                if b == 0:
                    if a == 0 or 0 < a < fplus:
                        send(src, a, 0, near(fstep, 1), 0)
                    if a == 0 or 0 < -a < fminus:
                        send(src, a, 0, near(fstep, -1), 1)
                    send(src, a, 0, near(sstep, 1), 2)
                    send(src, a, 0, near(sstep, -1), 3)
                elif 0 < b < splus:
                    send(src, a, b, near(sstep, 1), 2)
                elif 0 < -b < sminus:
                    send(src, a, b, near(sstep, -1), 3)
                send(src, a, b, partner, 4)

            for a in range(-fminus, fplus + 1):
                for b in range(-sminus, splus + 1):
                    levels.setdefault(abs(a) + abs(b), []).append((handle, a, b))

        for level in sorted(levels):
            for handle, a, b in levels[level]:
                handle(a, b, level > 0)
        for pi, (lo, n, sign, order) in enumerate(PIECES[1 - cc]):
            for yy in range(NY):
                for zz in range(NZ):
                    s = (yy * NZ + zz) * 2 + (1 - cc)
                    pltpu.make_async_remote_copy(
                        src_ref=g_ref.at[s, pl.ds(lo, n)], dst_ref=g_ref.at[s, pl.ds(lo, n)],
                        send_sem=sent.at[s, pi, 0], recv_sem=recv.at[s, pi], device_id=partner,
                        device_id_type=MESH).wait_recv()
        for cp in sends:
            cp.wait_send()

    @pl.when(c == 0)
    def _():
        role(0)

    @pl.when(c == 1)
    def _():
        role(1)

    for cp in owns:
        cp.wait()


def gather_env(left, right):
    shape = (NY * NZ * 2, 2 * left.shape[0]) + left.shape[1:]
    return pl.pallas_call(
        gather_kernel,
        out_shape=jax.ShapeDtypeStruct(shape, left.dtype),
        in_specs=[pl.BlockSpec(memory_space=pl.ANY)] * 2,
        out_specs=pl.BlockSpec(memory_space=pl.ANY),
        scratch_shapes=[
            pltpu.SemaphoreType.DMA((2,)),
            pltpu.SemaphoreType.DMA((NY * NZ * 2, 4)),
            pltpu.SemaphoreType.DMA((NY * NZ * 2, 4, 5)),
        ],
        compiler_params=pltpu.CompilerParams(collective_id=0, has_side_effects=True),
    )(left, right)


def block_kernel(lsec, rsec, owner, live, psi_ref, *refs):
    group = psi_ref.shape[0]
    width = psi_ref.shape[1]
    env_refs, out_ref = refs[:-1], refs[-1]
    rows = lax.broadcasted_iota(jnp.int32, (width, width), 0)
    cols = lax.broadcasted_iota(jnp.int32, (width, width), 1)
    for j in range(group):
        k = pl.program_id(0) * group + j
        l_ref, r_ref = env_refs[2 * j], env_refs[2 * j + 1]
        mask = (rows < live[lsec[k]]) & (cols < live[rsec[k]])
        masked = jnp.where(mask, psi_ref[j], jnp.zeros_like(psi_ref[j]))
        chans = l_ref.shape[1]
        lmat = l_ref[...].reshape(chans * width, width)
        y = jnp.dot(lmat, masked, preferred_element_type=jnp.float32).astype(jnp.bfloat16)
        ywide = jnp.concatenate([y[w * width:(w + 1) * width] for w in range(chans)], axis=1)
        rmat = r_ref[...].reshape(chans * width, width)
        acc = jnp.dot(ywide, rmat, preferred_element_type=jnp.float32)
        part = jnp.where(mask, acc, 0.0).astype(out_ref.dtype)
        share = out_ref.shape[2]
        for r in range(out_ref.shape[0]):
            out_ref[r, j] = part[r * share:(r + 1) * share]


def apply_blocks(psi, both, lsec, rsec, owner, live, nenv, group=8):
    count, width, _ = psi.shape
    share = width // nenv
    chans = both.shape[1] // 2
    env_specs = []
    for j in range(group):
        env_specs.append(pl.BlockSpec(
            (1, chans, width, width), lambda i, ls, rs, ow, lv, j=j: (ow[ls[i * group + j]], 0, 0, 0)))
        env_specs.append(pl.BlockSpec(
            (1, chans, width, width), lambda i, ls, rs, ow, lv, j=j: (ow[rs[i * group + j]], 1, 0, 0)))
    grid_spec = pltpu.PrefetchScalarGridSpec(
        num_scalar_prefetch=4,
        grid=(count // group,),
        in_specs=[pl.BlockSpec((group, width, width), lambda i, ls, rs, ow, lv: (i, 0, 0))] + env_specs,
        out_specs=pl.BlockSpec((nenv, group, share, width), lambda i, ls, rs, ow, lv: (0, i, 0, 0)),
    )
    flops = count * chans * 4 * width ** 3
    nbytes = count * (2 * chans + 2) * width * width * 2
    return pl.pallas_call(
        block_kernel,
        grid_spec=grid_spec,
        out_shape=jax.ShapeDtypeStruct((nenv, count, share, width), jnp.bfloat16),
        cost_estimate=pl.CostEstimate(flops=flops, bytes_accessed=nbytes, transcendentals=0),
    )(lsec, rsec, owner, live, psi, *([both] * (2 * group)))


def exchange_kernel(part_ref, out_ref, got, relay, own_sem, recv_sem, relay_sem, sent):
    nenv, count, share, width = part_ref.shape
    e = lax.axis_index("env")
    y = lax.axis_index("y")
    z = lax.axis_index("z")
    c = lax.axis_index("core")
    half = count // 2

    def at(d):
        return lax.rem(e + d + 2 * nenv, nenv)

    def dev(d):
        return (at(d), y, z, c)

    barrier = pltpu.get_barrier_semaphore()
    for d in (1, -1):
        pl.semaphore_signal(barrier, inc=1, device_id=dev(d), device_id_type=MESH)
    pl.semaphore_wait(barrier, 2)

    own = pltpu.make_async_copy(part_ref.at[e], got.at[e], own_sem)
    own.start()

    def remote(src, dst, rsem, ssem, d):
        return pltpu.make_async_remote_copy(
            src_ref=src, dst_ref=dst, send_sem=ssem, recv_sem=rsem,
            device_id=dev(d), device_id_type=MESH)

    lo, hi = pl.ds(0, half), pl.ds(half, half)
    sends = [
        remote(part_ref.at[at(1)], got.at[e], recv_sem.at[0], sent.at[0], 1),
        remote(part_ref.at[at(-1)], got.at[e], recv_sem.at[1], sent.at[1], -1),
        remote(part_ref.at[at(2), lo], relay.at[0], relay_sem.at[0], sent.at[2], 1),
        remote(part_ref.at[at(2), hi], relay.at[1], relay_sem.at[1], sent.at[3], -1),
    ]
    for cp in sends:
        cp.start()
    remote(relay.at[0], relay.at[0], relay_sem.at[0], sent.at[2], 1).wait_recv()
    fwd_up = remote(relay.at[0], got.at[at(-1), lo], recv_sem.at[2], sent.at[4], 1)
    fwd_up.start()
    remote(relay.at[1], relay.at[1], relay_sem.at[1], sent.at[3], -1).wait_recv()
    fwd_down = remote(relay.at[1], got.at[at(1), hi], recv_sem.at[3], sent.at[5], -1)
    fwd_down.start()
    remote(got.at[at(-1)], got.at[at(-1)], recv_sem.at[0], sent.at[0], -1).wait_recv()
    remote(got.at[at(1)], got.at[at(1)], recv_sem.at[1], sent.at[1], 1).wait_recv()
    remote(got.at[at(2), lo], got.at[at(2), lo], recv_sem.at[2], sent.at[4], -1).wait_recv()
    remote(got.at[at(2), hi], got.at[at(2), hi], recv_sem.at[3], sent.at[5], 1).wait_recv()
    own.wait()
    for cp in sends + [fwd_up, fwd_down]:
        cp.wait_send()

    def body(j, carry):
        total = got[0, j].astype(jnp.float32)
        for s in range(1, nenv):
            total = total + got[s, j].astype(jnp.float32)
        out_ref[j] = total.astype(out_ref.dtype)
        return carry

    lax.fori_loop(0, count, body, 0)


def exchange(part):
    nenv, count, share, width = part.shape
    return pl.pallas_call(
        exchange_kernel,
        out_shape=jax.ShapeDtypeStruct((count, share, width), part.dtype),
        in_specs=[pl.BlockSpec(memory_space=pl.ANY)],
        out_specs=pl.BlockSpec(memory_space=pltpu.VMEM),
        scratch_shapes=[
            pltpu.VMEM((nenv, count, share, width), part.dtype),
            pltpu.VMEM((2, count // 2, share, width), part.dtype),
            pltpu.SemaphoreType.DMA(()),
            pltpu.SemaphoreType.DMA((4,)),
            pltpu.SemaphoreType.DMA((2,)),
            pltpu.SemaphoreType.DMA((6,)),
        ],
        compiler_params=pltpu.CompilerParams(collective_id=1, has_side_effects=True),
    )(part)


def on_device(psi, left_env, right_env, left_sector, right_sector, sector_owner, sector_rows):
    nenv = lax.axis_size("env")
    count, width, _ = psi.shape
    lsec = left_sector[:, 0]
    rsec = right_sector[:, 0]
    both = gather_env(left_env[:, 0], right_env[:, 0])
    part = apply_blocks(psi, both, lsec, rsec, sector_owner, sector_rows, nenv)
    return exchange(part)


def solution(mesh):
    nenv, nwave = mesh.devices.shape
    split = jax.sharding.Mesh(mesh.devices.reshape(nenv, NY, NZ, 2), ("env", "y", "z", "core"))
    wave = ("y", "z", "core")
    return jax.shard_map(
        on_device,
        mesh=split,
        in_specs=(
            P(wave, None, None),
            P("env", wave, None, None),
            P("env", wave, None, None),
            P(wave, None),
            P(wave, None),
            P(),
            P(),
        ),
        out_specs=P(wave, "env", None),
        check_vma=False,
    )
```

```python
import functools

import jax
import jax.numpy as jnp
from jax import lax
from jax.experimental import pallas as pl
from jax.experimental.pallas import tpu as pltpu
from jax.sharding import PartitionSpec as P

MESH = pl.DeviceIdType.MESH
NY, NZ = 4, 8


PIECES = (
    ((0, 10, 1, "zy"), (10, 10, -1, "zy")),
    ((0, 8, 1, "yz"), (8, 2, 1, "zy"), (10, 8, -1, "yz"), (18, 2, -1, "zy")),
)


def gather_kernel(l_ref, r_ref, g_ref, own_sem, recv, sent):
    e = lax.axis_index("env")
    y = lax.axis_index("y")
    z = lax.axis_index("z")
    c = lax.axis_index("core")
    half = l_ref.shape[0]

    def dev(yy, zz, cc):
        return (e, lax.rem(yy + 2 * NY, NY), lax.rem(zz + 2 * NZ, NZ), cc)

    def slot(yy, zz, cc):
        return (lax.rem(yy + 2 * NY, NY) * NZ + lax.rem(zz + 2 * NZ, NZ)) * 2 + cc

    barrier = pltpu.get_barrier_semaphore()
    peers = [dev(y + 1, z, c), dev(y - 1, z, c), dev(y, z + 1, c), dev(y, z - 1, c), dev(y, z, 1 - c)]
    for p in peers:
        pl.semaphore_signal(barrier, inc=1, device_id=p, device_id_type=MESH)
    pl.semaphore_wait(barrier, len(peers))

    owns = []
    for h, src in enumerate((l_ref, r_ref)):
        cp = pltpu.make_async_copy(src, g_ref.at[slot(y, z, c), pl.ds(h * half, half)], own_sem.at[h])
        cp.start()
        owns.append(cp)

    def own_part(lo, n):
        if lo < half:
            return l_ref.at[pl.ds(lo, n)]
        return r_ref.at[pl.ds(lo - half, n)]

    zstep = lambda d: (0, d)
    ystep = lambda d: (d, 0)
    rings = {"z": (NZ, zstep), "y": (NY, ystep)}

    def role(cc):
        sends = []
        partner = dev(y, z, 1 - cc)
        levels = {}

        for pi, (lo, n, sign, order) in enumerate(PIECES[cc]):
            fsize, fstep = rings[order[0]]
            ssize, sstep = rings[order[1]]
            fplus, fminus = fsize // 2, fsize - 1 - fsize // 2
            splus, sminus = ssize // 2, ssize - 1 - ssize // 2

            def item(a, b, fstep=fstep, sstep=sstep, sign=sign):
                fy, fz = fstep(sign * a)
                sy, sz = sstep(sign * b)
                return slot(y - fy - sy, z - fz - sz, cc)

            def near(ring, d, sign=sign):
                dy, dz = ring(sign * d)
                return dev(y + dy, z + dz, cc)

            def send(src, a, b, target, kind, pi=pi, lo=lo, n=n, item=item):
                s = item(a, b)
                cp = pltpu.make_async_remote_copy(
                    src_ref=src, dst_ref=g_ref.at[s, pl.ds(lo, n)], send_sem=sent.at[s, pi, kind],
                    recv_sem=recv.at[s, pi], device_id=target, device_id_type=MESH)
                cp.start()
                sends.append(cp)

            def handle(a, b, wait, pi=pi, lo=lo, n=n, item=item, near=near, send=send,
                       fstep=fstep, sstep=sstep, fplus=fplus, fminus=fminus, splus=splus, sminus=sminus):
                if wait:
                    s = item(a, b)
                    pltpu.make_async_remote_copy(
                        src_ref=g_ref.at[s, pl.ds(lo, n)], dst_ref=g_ref.at[s, pl.ds(lo, n)],
                        send_sem=sent.at[s, pi, 0], recv_sem=recv.at[s, pi], device_id=partner,
                        device_id_type=MESH).wait_recv()
                    src = g_ref.at[s, pl.ds(lo, n)]
                else:
                    src = own_part(lo, n)
                if b == 0:
                    if a == 0 or 0 < a < fplus:
                        send(src, a, 0, near(fstep, 1), 0)
                    if a == 0 or 0 < -a < fminus:
                        send(src, a, 0, near(fstep, -1), 1)
                    send(src, a, 0, near(sstep, 1), 2)
                    send(src, a, 0, near(sstep, -1), 3)
                elif 0 < b < splus:
                    send(src, a, b, near(sstep, 1), 2)
                elif 0 < -b < sminus:
                    send(src, a, b, near(sstep, -1), 3)
                send(src, a, b, partner, 4)

            for a in range(-fminus, fplus + 1):
                for b in range(-sminus, splus + 1):
                    levels.setdefault(abs(a) + abs(b), []).append((handle, a, b))

        for level in sorted(levels):
            for handle, a, b in levels[level]:
                handle(a, b, level > 0)
        for pi, (lo, n, sign, order) in enumerate(PIECES[1 - cc]):
            for yy in range(NY):
                for zz in range(NZ):
                    s = (yy * NZ + zz) * 2 + (1 - cc)
                    pltpu.make_async_remote_copy(
                        src_ref=g_ref.at[s, pl.ds(lo, n)], dst_ref=g_ref.at[s, pl.ds(lo, n)],
                        send_sem=sent.at[s, pi, 0], recv_sem=recv.at[s, pi], device_id=partner,
                        device_id_type=MESH).wait_recv()
        for cp in sends:
            cp.wait_send()

    @pl.when(c == 0)
    def _():
        role(0)

    @pl.when(c == 1)
    def _():
        role(1)

    for cp in owns:
        cp.wait()


def gather_env(left, right):
    shape = (NY * NZ * 2, 2 * left.shape[0]) + left.shape[1:]
    return pl.pallas_call(
        gather_kernel,
        out_shape=jax.ShapeDtypeStruct(shape, left.dtype),
        in_specs=[pl.BlockSpec(memory_space=pl.ANY)] * 2,
        out_specs=pl.BlockSpec(memory_space=pl.ANY),
        scratch_shapes=[
            pltpu.SemaphoreType.DMA((2,)),
            pltpu.SemaphoreType.DMA((NY * NZ * 2, 4)),
            pltpu.SemaphoreType.DMA((NY * NZ * 2, 4, 5)),
        ],
        compiler_params=pltpu.CompilerParams(collective_id=0, has_side_effects=True),
    )(left, right)


def block_kernel(lsec, rsec, owner, live, psi_ref, *refs):
    group = psi_ref.shape[0]
    width = psi_ref.shape[1]
    env_refs, out_ref = refs[:-1], refs[-1]
    rows = lax.broadcasted_iota(jnp.int32, (width, width), 0)
    cols = lax.broadcasted_iota(jnp.int32, (width, width), 1)
    for j in range(group):
        k = pl.program_id(0) * group + j
        l_ref, r_ref = env_refs[2 * j], env_refs[2 * j + 1]
        mask = (rows < live[lsec[k]]) & (cols < live[rsec[k]])
        masked = jnp.where(mask, psi_ref[j], jnp.zeros_like(psi_ref[j]))
        chans = l_ref.shape[1]
        lmat = l_ref[...].reshape(chans * width, width)
        y = jnp.dot(lmat, masked, preferred_element_type=jnp.float32).astype(jnp.bfloat16)
        ywide = jnp.concatenate([y[w * width:(w + 1) * width] for w in range(chans)], axis=1)
        rmat = r_ref[...].reshape(chans * width, width)
        acc = jnp.dot(ywide, rmat, preferred_element_type=jnp.float32)
        part = jnp.where(mask, acc, 0.0).astype(out_ref.dtype)
        share = out_ref.shape[2]
        for r in range(out_ref.shape[0]):
            out_ref[r, j] = part[r * share:(r + 1) * share]


def apply_blocks(psi, both, lsec, rsec, owner, live, nenv, group=8):
    count, width, _ = psi.shape
    share = width // nenv
    chans = both.shape[1] // 2
    env_specs = []
    for j in range(group):
        env_specs.append(pl.BlockSpec(
            (1, chans, width, width), lambda i, ls, rs, ow, lv, j=j: (ow[ls[i * group + j]], 0, 0, 0)))
        env_specs.append(pl.BlockSpec(
            (1, chans, width, width), lambda i, ls, rs, ow, lv, j=j: (ow[rs[i * group + j]], 1, 0, 0)))
    grid_spec = pltpu.PrefetchScalarGridSpec(
        num_scalar_prefetch=4,
        grid=(count // group,),
        in_specs=[pl.BlockSpec((group, width, width), lambda i, ls, rs, ow, lv: (i, 0, 0))] + env_specs,
        out_specs=pl.BlockSpec((nenv, group, share, width), lambda i, ls, rs, ow, lv: (0, i, 0, 0)),
    )
    flops = count * chans * 4 * width ** 3
    nbytes = count * (2 * chans + 2) * width * width * 2
    return pl.pallas_call(
        block_kernel,
        grid_spec=grid_spec,
        out_shape=jax.ShapeDtypeStruct((nenv, count, share, width), jnp.bfloat16),
        cost_estimate=pl.CostEstimate(flops=flops, bytes_accessed=nbytes, transcendentals=0),
    )(lsec, rsec, owner, live, psi, *([both] * (2 * group)))


def exchange_kernel(part_ref, out_ref, got, relay, own_sem, recv_sem, relay_sem, sent):
    nenv, count, share, width = part_ref.shape
    e = lax.axis_index("env")
    y = lax.axis_index("y")
    z = lax.axis_index("z")
    c = lax.axis_index("core")
    half = count // 2

    def at(d):
        return lax.rem(e + d + 2 * nenv, nenv)

    def dev(d):
        return (at(d), y, z, c)

    barrier = pltpu.get_barrier_semaphore()
    for d in (1, -1):
        pl.semaphore_signal(barrier, inc=1, device_id=dev(d), device_id_type=MESH)
    pl.semaphore_wait(barrier, 2)

    own = pltpu.make_async_copy(part_ref.at[e], got.at[e], own_sem)
    own.start()

    def remote(src, dst, rsem, ssem, d):
        return pltpu.make_async_remote_copy(
            src_ref=src, dst_ref=dst, send_sem=ssem, recv_sem=rsem,
            device_id=dev(d), device_id_type=MESH)

    lo, hi = pl.ds(0, half), pl.ds(half, half)
    sends = [
        remote(part_ref.at[at(1)], got.at[e], recv_sem.at[0], sent.at[0], 1),
        remote(part_ref.at[at(-1)], got.at[e], recv_sem.at[1], sent.at[1], -1),
        remote(part_ref.at[at(2), lo], relay.at[0], relay_sem.at[0], sent.at[2], 1),
        remote(part_ref.at[at(2), hi], relay.at[1], relay_sem.at[1], sent.at[3], -1),
    ]
    for cp in sends:
        cp.start()
    remote(relay.at[0], relay.at[0], relay_sem.at[0], sent.at[2], 1).wait_recv()
    fwd_up = remote(relay.at[0], got.at[at(-1), lo], recv_sem.at[2], sent.at[4], 1)
    fwd_up.start()
    remote(relay.at[1], relay.at[1], relay_sem.at[1], sent.at[3], -1).wait_recv()
    fwd_down = remote(relay.at[1], got.at[at(1), hi], recv_sem.at[3], sent.at[5], -1)
    fwd_down.start()
    remote(got.at[at(-1)], got.at[at(-1)], recv_sem.at[0], sent.at[0], -1).wait_recv()
    remote(got.at[at(1)], got.at[at(1)], recv_sem.at[1], sent.at[1], 1).wait_recv()
    remote(got.at[at(2), lo], got.at[at(2), lo], recv_sem.at[2], sent.at[4], -1).wait_recv()
    remote(got.at[at(2), hi], got.at[at(2), hi], recv_sem.at[3], sent.at[5], 1).wait_recv()
    own.wait()
    for cp in sends + [fwd_up, fwd_down]:
        cp.wait_send()

    out_ref[...] = got[...]


def exchange(part):
    nenv, count, share, width = part.shape
    return pl.pallas_call(
        exchange_kernel,
        out_shape=jax.ShapeDtypeStruct((nenv, count, share, width), part.dtype),
        in_specs=[pl.BlockSpec(memory_space=pl.ANY)],
        out_specs=pl.BlockSpec(memory_space=pltpu.VMEM),
        scratch_shapes=[
            pltpu.VMEM((nenv, count, share, width), part.dtype),
            pltpu.VMEM((2, count // 2, share, width), part.dtype),
            pltpu.SemaphoreType.DMA(()),
            pltpu.SemaphoreType.DMA((4,)),
            pltpu.SemaphoreType.DMA((2,)),
            pltpu.SemaphoreType.DMA((6,)),
        ],
        compiler_params=pltpu.CompilerParams(collective_id=1, has_side_effects=True),
    )(part)


def on_device(psi, left_env, right_env, left_sector, right_sector, sector_owner, sector_rows):
    nenv = lax.axis_size("env")
    count, width, _ = psi.shape
    lsec = left_sector[:, 0]
    rsec = right_sector[:, 0]
    both = gather_env(left_env[:, 0], right_env[:, 0])
    part = apply_blocks(psi, both, lsec, rsec, sector_owner, sector_rows, nenv)
    got = exchange(part)
    return jnp.sum(got.astype(jnp.float32), axis=0).astype(jnp.bfloat16)


def solution(mesh):
    nenv, nwave = mesh.devices.shape
    split = jax.sharding.Mesh(mesh.devices.reshape(nenv, NY, NZ, 2), ("env", "y", "z", "core"))
    wave = ("y", "z", "core")
    return jax.shard_map(
        on_device,
        mesh=split,
        in_specs=(
            P(wave, None, None),
            P("env", wave, None, None),
            P("env", wave, None, None),
            P(wave, None),
            P(wave, None),
            P(),
            P(),
        ),
        out_specs=P(wave, "env", None),
        check_vma=False,
    )
```

```python
import functools

import jax
import jax.numpy as jnp
from jax import lax
from jax.experimental import pallas as pl
from jax.experimental.pallas import tpu as pltpu
from jax.sharding import PartitionSpec as P

MESH = pl.DeviceIdType.MESH
NY, NZ = 4, 8


PIECES = (
    ((0, 10, 1, "zy"), (10, 10, -1, "zy")),
    ((0, 8, 1, "yz"), (8, 2, 1, "zy"), (10, 8, -1, "yz"), (18, 2, -1, "zy")),
)


def gather_kernel(l_ref, r_ref, g_ref, own_sem, recv, sent):
    e = lax.axis_index("env")
    y = lax.axis_index("y")
    z = lax.axis_index("z")
    c = lax.axis_index("core")
    half = l_ref.shape[0]

    def dev(yy, zz, cc):
        return (e, lax.rem(yy + 2 * NY, NY), lax.rem(zz + 2 * NZ, NZ), cc)

    def slot(yy, zz, cc):
        return (lax.rem(yy + 2 * NY, NY) * NZ + lax.rem(zz + 2 * NZ, NZ)) * 2 + cc

    barrier = pltpu.get_barrier_semaphore()
    peers = [dev(y + 1, z, c), dev(y - 1, z, c), dev(y, z + 1, c), dev(y, z - 1, c), dev(y, z, 1 - c)]
    for p in peers:
        pl.semaphore_signal(barrier, inc=1, device_id=p, device_id_type=MESH)
    pl.semaphore_wait(barrier, len(peers))

    owns = []
    for h, src in enumerate((l_ref, r_ref)):
        cp = pltpu.make_async_copy(src, g_ref.at[slot(y, z, c), pl.ds(h * half, half)], own_sem.at[h])
        cp.start()
        owns.append(cp)

    def own_part(lo, n):
        if lo < half:
            return l_ref.at[pl.ds(lo, n)]
        return r_ref.at[pl.ds(lo - half, n)]

    zstep = lambda d: (0, d)
    ystep = lambda d: (d, 0)
    rings = {"z": (NZ, zstep), "y": (NY, ystep)}

    def role(cc):
        sends = []
        partner = dev(y, z, 1 - cc)
        levels = {}

        for pi, (lo, n, sign, order) in enumerate(PIECES[cc]):
            fsize, fstep = rings[order[0]]
            ssize, sstep = rings[order[1]]
            fplus, fminus = fsize // 2, fsize - 1 - fsize // 2
            splus, sminus = ssize // 2, ssize - 1 - ssize // 2

            def item(a, b, fstep=fstep, sstep=sstep, sign=sign):
                fy, fz = fstep(sign * a)
                sy, sz = sstep(sign * b)
                return slot(y - fy - sy, z - fz - sz, cc)

            def near(ring, d, sign=sign):
                dy, dz = ring(sign * d)
                return dev(y + dy, z + dz, cc)

            def send(src, a, b, target, kind, pi=pi, lo=lo, n=n, item=item):
                s = item(a, b)
                cp = pltpu.make_async_remote_copy(
                    src_ref=src, dst_ref=g_ref.at[s, pl.ds(lo, n)], send_sem=sent.at[s, pi, kind],
                    recv_sem=recv.at[s, pi], device_id=target, device_id_type=MESH)
                cp.start()
                sends.append(cp)

            def handle(a, b, wait, pi=pi, lo=lo, n=n, item=item, near=near, send=send,
                       fstep=fstep, sstep=sstep, fplus=fplus, fminus=fminus, splus=splus, sminus=sminus):
                if wait:
                    s = item(a, b)
                    pltpu.make_async_remote_copy(
                        src_ref=g_ref.at[s, pl.ds(lo, n)], dst_ref=g_ref.at[s, pl.ds(lo, n)],
                        send_sem=sent.at[s, pi, 0], recv_sem=recv.at[s, pi], device_id=partner,
                        device_id_type=MESH).wait_recv()
                    src = g_ref.at[s, pl.ds(lo, n)]
                else:
                    src = own_part(lo, n)
                if b == 0:
                    if a == 0 or 0 < a < fplus:
                        send(src, a, 0, near(fstep, 1), 0)
                    if a == 0 or 0 < -a < fminus:
                        send(src, a, 0, near(fstep, -1), 1)
                    send(src, a, 0, near(sstep, 1), 2)
                    send(src, a, 0, near(sstep, -1), 3)
                elif 0 < b < splus:
                    send(src, a, b, near(sstep, 1), 2)
                elif 0 < -b < sminus:
                    send(src, a, b, near(sstep, -1), 3)
                send(src, a, b, partner, 4)

            for a in range(-fminus, fplus + 1):
                for b in range(-sminus, splus + 1):
                    levels.setdefault(abs(a) + abs(b), []).append((handle, a, b))

        for level in sorted(levels):
            for handle, a, b in levels[level]:
                handle(a, b, level > 0)
        for pi, (lo, n, sign, order) in enumerate(PIECES[1 - cc]):
            for yy in range(NY):
                for zz in range(NZ):
                    s = (yy * NZ + zz) * 2 + (1 - cc)
                    pltpu.make_async_remote_copy(
                        src_ref=g_ref.at[s, pl.ds(lo, n)], dst_ref=g_ref.at[s, pl.ds(lo, n)],
                        send_sem=sent.at[s, pi, 0], recv_sem=recv.at[s, pi], device_id=partner,
                        device_id_type=MESH).wait_recv()
        for cp in sends:
            cp.wait_send()

    @pl.when(c == 0)
    def _():
        role(0)

    @pl.when(c == 1)
    def _():
        role(1)

    for cp in owns:
        cp.wait()


def gather_env(left, right):
    shape = (NY * NZ * 2, 2 * left.shape[0]) + left.shape[1:]
    return pl.pallas_call(
        gather_kernel,
        out_shape=jax.ShapeDtypeStruct(shape, left.dtype),
        in_specs=[pl.BlockSpec(memory_space=pl.ANY)] * 2,
        out_specs=pl.BlockSpec(memory_space=pl.ANY),
        scratch_shapes=[
            pltpu.SemaphoreType.DMA((2,)),
            pltpu.SemaphoreType.DMA((NY * NZ * 2, 4)),
            pltpu.SemaphoreType.DMA((NY * NZ * 2, 4, 5)),
        ],
        compiler_params=pltpu.CompilerParams(collective_id=0, has_side_effects=True),
    )(left, right)


def block_kernel(lsec, rsec, owner, live, psi_ref, *refs):
    group = psi_ref.shape[0]
    width = psi_ref.shape[1]
    env_refs, out_ref = refs[:-1], refs[-1]
    rows = lax.broadcasted_iota(jnp.int32, (width, width), 0)
    cols = lax.broadcasted_iota(jnp.int32, (width, width), 1)
    for j in range(group):
        k = pl.program_id(0) * group + j
        l_ref, r_ref = env_refs[2 * j], env_refs[2 * j + 1]
        mask = (rows < live[lsec[k]]) & (cols < live[rsec[k]])
        masked = jnp.where(mask, psi_ref[j], jnp.zeros_like(psi_ref[j]))
        chans = l_ref.shape[1]
        lmat = l_ref[...].reshape(chans * width, width)
        y = jnp.dot(lmat, masked, preferred_element_type=jnp.float32).astype(jnp.bfloat16)
        ywide = jnp.concatenate([y[w * width:(w + 1) * width] for w in range(chans)], axis=1)
        rmat = r_ref[...].reshape(chans * width, width)
        acc = jnp.dot(ywide, rmat, preferred_element_type=jnp.float32)
        part = jnp.where(mask, acc, 0.0).astype(out_ref.dtype)
        share = out_ref.shape[2]
        for r in range(out_ref.shape[0]):
            out_ref[r, j] = part[r * share:(r + 1) * share]


def apply_blocks(psi, both, lsec, rsec, owner, live, nenv, group=16):
    count, width, _ = psi.shape
    share = width // nenv
    chans = both.shape[1] // 2
    env_specs = []
    for j in range(group):
        env_specs.append(pl.BlockSpec(
            (1, chans, width, width), lambda i, ls, rs, ow, lv, j=j: (ow[ls[i * group + j]], 0, 0, 0)))
        env_specs.append(pl.BlockSpec(
            (1, chans, width, width), lambda i, ls, rs, ow, lv, j=j: (ow[rs[i * group + j]], 1, 0, 0)))
    grid_spec = pltpu.PrefetchScalarGridSpec(
        num_scalar_prefetch=4,
        grid=(count // group,),
        in_specs=[pl.BlockSpec((group, width, width), lambda i, ls, rs, ow, lv: (i, 0, 0))] + env_specs,
        out_specs=pl.BlockSpec((nenv, group, share, width), lambda i, ls, rs, ow, lv: (0, i, 0, 0)),
    )
    flops = count * chans * 4 * width ** 3
    nbytes = count * (2 * chans + 2) * width * width * 2
    return pl.pallas_call(
        block_kernel,
        grid_spec=grid_spec,
        out_shape=jax.ShapeDtypeStruct((nenv, count, share, width), jnp.bfloat16),
        cost_estimate=pl.CostEstimate(flops=flops, bytes_accessed=nbytes, transcendentals=0),
    )(lsec, rsec, owner, live, psi, *([both] * (2 * group)))


def exchange_kernel(part_ref, out_ref, got, relay, own_sem, recv_sem, relay_sem, sent):
    nenv, count, share, width = part_ref.shape
    e = lax.axis_index("env")
    y = lax.axis_index("y")
    z = lax.axis_index("z")
    c = lax.axis_index("core")
    half = count // 2

    def at(d):
        return lax.rem(e + d + 2 * nenv, nenv)

    def dev(d):
        return (at(d), y, z, c)

    barrier = pltpu.get_barrier_semaphore()
    for d in (1, -1):
        pl.semaphore_signal(barrier, inc=1, device_id=dev(d), device_id_type=MESH)
    pl.semaphore_wait(barrier, 2)

    own = pltpu.make_async_copy(part_ref.at[e], got.at[e], own_sem)
    own.start()

    def remote(src, dst, rsem, ssem, d):
        return pltpu.make_async_remote_copy(
            src_ref=src, dst_ref=dst, send_sem=ssem, recv_sem=rsem,
            device_id=dev(d), device_id_type=MESH)

    lo, hi = pl.ds(0, half), pl.ds(half, half)
    sends = [
        remote(part_ref.at[at(1)], got.at[e], recv_sem.at[0], sent.at[0], 1),
        remote(part_ref.at[at(-1)], got.at[e], recv_sem.at[1], sent.at[1], -1),
        remote(part_ref.at[at(2), lo], relay.at[0], relay_sem.at[0], sent.at[2], 1),
        remote(part_ref.at[at(2), hi], relay.at[1], relay_sem.at[1], sent.at[3], -1),
    ]
    for cp in sends:
        cp.start()
    remote(relay.at[0], relay.at[0], relay_sem.at[0], sent.at[2], 1).wait_recv()
    fwd_up = remote(relay.at[0], got.at[at(-1), lo], recv_sem.at[2], sent.at[4], 1)
    fwd_up.start()
    remote(relay.at[1], relay.at[1], relay_sem.at[1], sent.at[3], -1).wait_recv()
    fwd_down = remote(relay.at[1], got.at[at(1), hi], recv_sem.at[3], sent.at[5], -1)
    fwd_down.start()
    remote(got.at[at(-1)], got.at[at(-1)], recv_sem.at[0], sent.at[0], -1).wait_recv()
    remote(got.at[at(1)], got.at[at(1)], recv_sem.at[1], sent.at[1], 1).wait_recv()
    remote(got.at[at(2), lo], got.at[at(2), lo], recv_sem.at[2], sent.at[4], -1).wait_recv()
    remote(got.at[at(2), hi], got.at[at(2), hi], recv_sem.at[3], sent.at[5], 1).wait_recv()
    own.wait()
    for cp in sends + [fwd_up, fwd_down]:
        cp.wait_send()

    def body(j, carry):
        total = got[0, j].astype(jnp.float32)
        for s in range(1, nenv):
            total = total + got[s, j].astype(jnp.float32)
        out_ref[j] = total.astype(out_ref.dtype)
        return carry

    lax.fori_loop(0, count, body, 0)


def exchange(part):
    nenv, count, share, width = part.shape
    return pl.pallas_call(
        exchange_kernel,
        out_shape=jax.ShapeDtypeStruct((count, share, width), part.dtype),
        in_specs=[pl.BlockSpec(memory_space=pl.ANY)],
        out_specs=pl.BlockSpec(memory_space=pltpu.VMEM),
        scratch_shapes=[
            pltpu.VMEM((nenv, count, share, width), part.dtype),
            pltpu.VMEM((2, count // 2, share, width), part.dtype),
            pltpu.SemaphoreType.DMA(()),
            pltpu.SemaphoreType.DMA((4,)),
            pltpu.SemaphoreType.DMA((2,)),
            pltpu.SemaphoreType.DMA((6,)),
        ],
        compiler_params=pltpu.CompilerParams(collective_id=1, has_side_effects=True),
    )(part)


def on_device(psi, left_env, right_env, left_sector, right_sector, sector_owner, sector_rows):
    nenv = lax.axis_size("env")
    count, width, _ = psi.shape
    lsec = left_sector[:, 0]
    rsec = right_sector[:, 0]
    both = gather_env(left_env[:, 0], right_env[:, 0])
    part = apply_blocks(psi, both, lsec, rsec, sector_owner, sector_rows, nenv)
    return exchange(part)


def solution(mesh):
    nenv, nwave = mesh.devices.shape
    split = jax.sharding.Mesh(mesh.devices.reshape(nenv, NY, NZ, 2), ("env", "y", "z", "core"))
    wave = ("y", "z", "core")
    return jax.shard_map(
        on_device,
        mesh=split,
        in_specs=(
            P(wave, None, None),
            P("env", wave, None, None),
            P("env", wave, None, None),
            P(wave, None),
            P(wave, None),
            P(),
            P(),
        ),
        out_specs=P(wave, "env", None),
        check_vma=False,
    )
```

```python
import functools

import jax
import jax.numpy as jnp
from jax import lax
from jax.experimental import pallas as pl
from jax.experimental.pallas import tpu as pltpu
from jax.sharding import PartitionSpec as P

MESH = pl.DeviceIdType.MESH
NY, NZ = 4, 8


PIECES = (
    ((0, 10, 1, "zy"), (10, 10, -1, "zy")),
    ((0, 8, 1, "yz"), (8, 2, 1, "zy"), (10, 8, -1, "yz"), (18, 2, -1, "zy")),
)


def gather_kernel(l_ref, r_ref, g_ref, own_sem, recv, sent):
    e = lax.axis_index("env")
    y = lax.axis_index("y")
    z = lax.axis_index("z")
    c = lax.axis_index("core")
    half = l_ref.shape[0]

    def dev(yy, zz, cc):
        return (e, lax.rem(yy + 2 * NY, NY), lax.rem(zz + 2 * NZ, NZ), cc)

    def slot(yy, zz, cc):
        return (lax.rem(yy + 2 * NY, NY) * NZ + lax.rem(zz + 2 * NZ, NZ)) * 2 + cc

    barrier = pltpu.get_barrier_semaphore()
    peers = [dev(y + 1, z, c), dev(y - 1, z, c), dev(y, z + 1, c), dev(y, z - 1, c), dev(y, z, 1 - c)]
    for p in peers:
        pl.semaphore_signal(barrier, inc=1, device_id=p, device_id_type=MESH)
    pl.semaphore_wait(barrier, len(peers))

    owns = []
    for h, src in enumerate((l_ref, r_ref)):
        cp = pltpu.make_async_copy(src, g_ref.at[slot(y, z, c), pl.ds(h * half, half)], own_sem.at[h])
        cp.start()
        owns.append(cp)

    def own_part(lo, n):
        if lo < half:
            return l_ref.at[pl.ds(lo, n)]
        return r_ref.at[pl.ds(lo - half, n)]

    zstep = lambda d: (0, d)
    ystep = lambda d: (d, 0)
    rings = {"z": (NZ, zstep), "y": (NY, ystep)}

    def role(cc):
        sends = []
        partner = dev(y, z, 1 - cc)
        levels = {}

        for pi, (lo, n, sign, order) in enumerate(PIECES[cc]):
            fsize, fstep = rings[order[0]]
            ssize, sstep = rings[order[1]]
            fplus, fminus = fsize // 2, fsize - 1 - fsize // 2
            splus, sminus = ssize // 2, ssize - 1 - ssize // 2

            def item(a, b, fstep=fstep, sstep=sstep, sign=sign):
                fy, fz = fstep(sign * a)
                sy, sz = sstep(sign * b)
                return slot(y - fy - sy, z - fz - sz, cc)

            def near(ring, d, sign=sign):
                dy, dz = ring(sign * d)
                return dev(y + dy, z + dz, cc)

            def send(src, a, b, target, kind, pi=pi, lo=lo, n=n, item=item):
                s = item(a, b)
                cp = pltpu.make_async_remote_copy(
                    src_ref=src, dst_ref=g_ref.at[s, pl.ds(lo, n)], send_sem=sent.at[s, pi, kind],
                    recv_sem=recv.at[s, pi], device_id=target, device_id_type=MESH)
                cp.start()
                sends.append(cp)

            def handle(a, b, wait, pi=pi, lo=lo, n=n, item=item, near=near, send=send,
                       fstep=fstep, sstep=sstep, fplus=fplus, fminus=fminus, splus=splus, sminus=sminus):
                if wait:
                    s = item(a, b)
                    pltpu.make_async_remote_copy(
                        src_ref=g_ref.at[s, pl.ds(lo, n)], dst_ref=g_ref.at[s, pl.ds(lo, n)],
                        send_sem=sent.at[s, pi, 0], recv_sem=recv.at[s, pi], device_id=partner,
                        device_id_type=MESH).wait_recv()
                    src = g_ref.at[s, pl.ds(lo, n)]
                else:
                    src = own_part(lo, n)
                if b == 0:
                    if a == 0 or 0 < a < fplus:
                        send(src, a, 0, near(fstep, 1), 0)
                    if a == 0 or 0 < -a < fminus:
                        send(src, a, 0, near(fstep, -1), 1)
                    send(src, a, 0, near(sstep, 1), 2)
                    send(src, a, 0, near(sstep, -1), 3)
                elif 0 < b < splus:
                    send(src, a, b, near(sstep, 1), 2)
                elif 0 < -b < sminus:
                    send(src, a, b, near(sstep, -1), 3)
                send(src, a, b, partner, 4)

            for a in range(-fminus, fplus + 1):
                for b in range(-sminus, splus + 1):
                    levels.setdefault(abs(a) + abs(b), []).append((handle, a, b))

        for level in sorted(levels):
            for handle, a, b in levels[level]:
                handle(a, b, level > 0)
        for pi, (lo, n, sign, order) in enumerate(PIECES[1 - cc]):
            for yy in range(NY):
                for zz in range(NZ):
                    s = (yy * NZ + zz) * 2 + (1 - cc)
                    pltpu.make_async_remote_copy(
                        src_ref=g_ref.at[s, pl.ds(lo, n)], dst_ref=g_ref.at[s, pl.ds(lo, n)],
                        send_sem=sent.at[s, pi, 0], recv_sem=recv.at[s, pi], device_id=partner,
                        device_id_type=MESH).wait_recv()
        for cp in sends:
            cp.wait_send()

    @pl.when(c == 0)
    def _():
        role(0)

    @pl.when(c == 1)
    def _():
        role(1)

    for cp in owns:
        cp.wait()


def gather_env(left, right):
    shape = (NY * NZ * 2, 2 * left.shape[0]) + left.shape[1:]
    return pl.pallas_call(
        gather_kernel,
        out_shape=jax.ShapeDtypeStruct(shape, left.dtype),
        in_specs=[pl.BlockSpec(memory_space=pl.ANY)] * 2,
        out_specs=pl.BlockSpec(memory_space=pl.ANY),
        scratch_shapes=[
            pltpu.SemaphoreType.DMA((2,)),
            pltpu.SemaphoreType.DMA((NY * NZ * 2, 4)),
            pltpu.SemaphoreType.DMA((NY * NZ * 2, 4, 5)),
        ],
        compiler_params=pltpu.CompilerParams(collective_id=0, has_side_effects=True),
    )(left, right)


def block_kernel(lsec, rsec, owner, live, psi_ref, *refs):
    group = psi_ref.shape[0]
    width = psi_ref.shape[1]
    env_refs, out_ref = refs[:-1], refs[-1]
    rows = lax.broadcasted_iota(jnp.int32, (width, width), 0)
    cols = lax.broadcasted_iota(jnp.int32, (width, width), 1)
    for j in range(group):
        k = pl.program_id(0) * group + j
        l_ref, r_ref = env_refs[2 * j], env_refs[2 * j + 1]
        mask = (rows < live[lsec[k]]) & (cols < live[rsec[k]])
        masked = jnp.where(mask, psi_ref[j], jnp.zeros_like(psi_ref[j]))
        chans = l_ref.shape[1]
        lmat = l_ref[...].reshape(chans * width, width)
        y = jnp.dot(lmat, masked, preferred_element_type=jnp.float32).astype(jnp.bfloat16)
        ywide = jnp.concatenate([y[w * width:(w + 1) * width] for w in range(chans)], axis=1)
        rmat = r_ref[...].reshape(chans * width, width)
        acc = jnp.dot(ywide, rmat, preferred_element_type=jnp.float32)
        part = jnp.where(mask, acc, 0.0).astype(out_ref.dtype)
        share = out_ref.shape[2]
        for r in range(out_ref.shape[0]):
            out_ref[r, j] = part[r * share:(r + 1) * share]


def apply_blocks(psi, both, lsec, rsec, owner, live, nenv, group=8):
    count, width, _ = psi.shape
    share = width // nenv
    chans = both.shape[1] // 2
    env_specs = []
    for j in range(group):
        env_specs.append(pl.BlockSpec(
            (1, chans, width, width), lambda i, ls, rs, ow, lv, j=j: (ow[ls[i * group + j]], 0, 0, 0)))
        env_specs.append(pl.BlockSpec(
            (1, chans, width, width), lambda i, ls, rs, ow, lv, j=j: (ow[rs[i * group + j]], 1, 0, 0)))
    grid_spec = pltpu.PrefetchScalarGridSpec(
        num_scalar_prefetch=4,
        grid=(count // group,),
        in_specs=[pl.BlockSpec((group, width, width), lambda i, ls, rs, ow, lv: (i, 0, 0))] + env_specs,
        out_specs=pl.BlockSpec((nenv, group, share, width), lambda i, ls, rs, ow, lv: (0, i, 0, 0)),
    )
    flops = count * chans * 4 * width ** 3
    nbytes = count * (2 * chans + 2) * width * width * 2
    return pl.pallas_call(
        block_kernel,
        grid_spec=grid_spec,
        out_shape=jax.ShapeDtypeStruct((nenv, count, share, width), jnp.bfloat16),
        cost_estimate=pl.CostEstimate(flops=flops, bytes_accessed=nbytes, transcendentals=0),
    )(lsec, rsec, owner, live, psi, *([both] * (2 * group)))


def exchange_kernel(part_ref, out_ref, got, relay, own_sem, recv_sem, relay_sem, sent):
    nenv, count, share, width = part_ref.shape
    e = lax.axis_index("env")
    y = lax.axis_index("y")
    z = lax.axis_index("z")
    c = lax.axis_index("core")
    half = count // 2

    def at(d):
        return lax.rem(e + d + 2 * nenv, nenv)

    def dev(d):
        return (at(d), y, z, c)

    barrier = pltpu.get_barrier_semaphore()
    for d in (1, -1):
        pl.semaphore_signal(barrier, inc=1, device_id=dev(d), device_id_type=MESH)
    pl.semaphore_wait(barrier, 2)

    own = pltpu.make_async_copy(part_ref.at[e], got.at[e], own_sem)
    own.start()

    def remote(src, dst, rsem, ssem, d):
        return pltpu.make_async_remote_copy(
            src_ref=src, dst_ref=dst, send_sem=ssem, recv_sem=rsem,
            device_id=dev(d), device_id_type=MESH)

    lo, hi = pl.ds(0, half), pl.ds(half, half)
    sends = [
        remote(part_ref.at[at(1)], got.at[e], recv_sem.at[0], sent.at[0], 1),
        remote(part_ref.at[at(-1)], got.at[e], recv_sem.at[1], sent.at[1], -1),
        remote(part_ref.at[at(2), lo], relay.at[0], relay_sem.at[0], sent.at[2], 1),
        remote(part_ref.at[at(2), hi], relay.at[1], relay_sem.at[1], sent.at[3], -1),
    ]
    for cp in sends:
        cp.start()
    remote(relay.at[0], relay.at[0], relay_sem.at[0], sent.at[2], 1).wait_recv()
    fwd_up = remote(relay.at[0], got.at[at(-1), lo], recv_sem.at[2], sent.at[4], 1)
    fwd_up.start()
    remote(relay.at[1], relay.at[1], relay_sem.at[1], sent.at[3], -1).wait_recv()
    fwd_down = remote(relay.at[1], got.at[at(1), hi], recv_sem.at[3], sent.at[5], -1)
    fwd_down.start()
    remote(got.at[at(-1)], got.at[at(-1)], recv_sem.at[0], sent.at[0], -1).wait_recv()
    remote(got.at[at(1)], got.at[at(1)], recv_sem.at[1], sent.at[1], 1).wait_recv()
    remote(got.at[at(2), lo], got.at[at(2), lo], recv_sem.at[2], sent.at[4], -1).wait_recv()
    remote(got.at[at(2), hi], got.at[at(2), hi], recv_sem.at[3], sent.at[5], 1).wait_recv()
    own.wait()
    for cp in sends + [fwd_up, fwd_down]:
        cp.wait_send()

    step = 8

    def body(j, carry):
        blocks = pl.ds(pl.multiple_of(j * step, step), step)
        total = got[0, blocks].astype(jnp.float32)
        for s in range(1, nenv):
            total = total + got[s, blocks].astype(jnp.float32)
        out_ref[blocks] = total.astype(out_ref.dtype)
        return carry

    lax.fori_loop(0, count // step, body, 0)


def exchange(part):
    nenv, count, share, width = part.shape
    return pl.pallas_call(
        exchange_kernel,
        out_shape=jax.ShapeDtypeStruct((count, share, width), part.dtype),
        in_specs=[pl.BlockSpec(memory_space=pl.ANY)],
        out_specs=pl.BlockSpec(memory_space=pltpu.VMEM),
        scratch_shapes=[
            pltpu.VMEM((nenv, count, share, width), part.dtype),
            pltpu.VMEM((2, count // 2, share, width), part.dtype),
            pltpu.SemaphoreType.DMA(()),
            pltpu.SemaphoreType.DMA((4,)),
            pltpu.SemaphoreType.DMA((2,)),
            pltpu.SemaphoreType.DMA((6,)),
        ],
        compiler_params=pltpu.CompilerParams(collective_id=1, has_side_effects=True),
    )(part)


def on_device(psi, left_env, right_env, left_sector, right_sector, sector_owner, sector_rows):
    nenv = lax.axis_size("env")
    count, width, _ = psi.shape
    lsec = left_sector[:, 0]
    rsec = right_sector[:, 0]
    both = gather_env(left_env[:, 0], right_env[:, 0])
    part = apply_blocks(psi, both, lsec, rsec, sector_owner, sector_rows, nenv)
    return exchange(part)


def solution(mesh):
    nenv, nwave = mesh.devices.shape
    split = jax.sharding.Mesh(mesh.devices.reshape(nenv, NY, NZ, 2), ("env", "y", "z", "core"))
    wave = ("y", "z", "core")
    return jax.shard_map(
        on_device,
        mesh=split,
        in_specs=(
            P(wave, None, None),
            P("env", wave, None, None),
            P("env", wave, None, None),
            P(wave, None),
            P(wave, None),
            P(),
            P(),
        ),
        out_specs=P(wave, "env", None),
        check_vma=False,
    )
```
